512 devices in a mesh: probe: 16 (over y, x), space: 32 (over z, core).
Axes of the slice: x: 4, y: 4, z: 16, core: 2. Of those that a mesh axis runs over, the one named last changes fastest.
Arguments:
- probes: float32 [128, 131072], P('probe', 'space'), may hold values from -6 to 6
- sensitivity: float32 [8, 8, 65536], P(None, None, 'space'), may hold values from -2.1 to 2.1
- obs_weight: float32 [8, 65536], P(None, 'space'), may hold values from 0.5 to 4
- prior_weight: float32 [131072], P('space'), may hold values from 0.2 to 2
- connectivity: int32 [8, 65536], P(None, 'space'), may hold values from 0 to 4351, as said below
Outputs:
- basis: float32 [128, 131072], P('probe', 'space')
- factor: float32 [128, 128], replicated
The draws below stay inside these ranges and needn't reach their ends.
Inputs may be any that keep to these rules, and one draw needn't show every extreme that they name: Each column holds 8 distinct numbers. For an element of the block of device d of space (columns d * 2048 to (d + 1) * 2048 - 1), connectivity + d * 4096 - 128 is an existing node, and the values 0 and 4351 are both named wherever those nodes exist.
All inputs are finite; a program needn't handle non-finite values.
Results may differ from the reference program's by a relative error of at most 0.0003.
Values sent between devices are 32-bit elements; how exact they have to be, the bound alone decides.
No kernel may reach another device: no remote copies, remote signals or barrier semaphores. Data moves between devices by JAX's collectives and lax.ppermute only.
A program may use at most 64 MiB of HBM per device.

```python
import math
import jax
import jax.numpy as jnp
from jax import lax

K = 128
ND = 4096
ED = 2048
HALO = 128
GAUSS = 8
NPE = 8
NODES = 131072
ELEMS = 65536


def draw_probes(key, part):
    group_count = K // 16
    key_shared = jax.random.fold_in(key, 11)
    key_scales = jax.random.fold_in(key, 12)
    key_jitter = jax.random.fold_in(key, 13)
    shared = jnp.clip(jax.random.normal(key_shared, (group_count, NODES), jnp.float32), -4.0, 4.0)
    scales = jax.random.uniform(key_scales, (K,), jnp.float32, 0.6, 1.4)
    perturb = jnp.clip(jax.random.normal(key_jitter, (K, NODES), jnp.float32), -4.0, 4.0)
    row_group = jnp.arange(K, dtype=jnp.int32) % group_count
    picked = shared[row_group]
    return (scales[:, None] * picked + 0.01 * perturb).astype(jnp.float32)


def draw_connectivity(key, part):
    element = jnp.arange(ELEMS, dtype=jnp.int32)
    device = element // ED
    local = element - device * ED
    stride = ND // ED
    base_low = device * ND + local * stride
    base_high = base_low + stride
    width = HALO // 4
    slot = jnp.arange(NPE, dtype=jnp.int32)[:, None]
    jitter = jax.random.randint(key, (NPE, ELEMS), 0, width, dtype=jnp.int32)
    jitter = jnp.where((slot == 0) & (local[None, :] == 0), 0, jitter)
    jitter = jnp.where((slot == NPE - 1) & (local[None, :] == ED - 1), width - 1, jitter)
    low_node = base_low[None, :] + slot * width + jitter - HALO
    high_node = base_high[None, :] + (slot - 4) * width + jitter
    node = jnp.where(slot < 4, low_node, high_node)
    node = jnp.where(node < 0, node + 4 * HALO, node)
    node = jnp.where(node >= NODES, node - 4 * HALO, node)
    offsets = device * ND - HALO
    return (node - offsets[None, :]).astype(jnp.int32)


def shard_levels(stream_key, dims, pieces, low, high):
    level, own = 1.0, jax.random.fold_in(stream_key, 6)
    for position, blocks in pieces:
        draws = jnp.exp(jax.random.uniform(jax.random.fold_in(own, position), (blocks,), jnp.float32, low / len(pieces), high / len(pieces)))
        level = level * jnp.repeat(draws, dims[position] // blocks).reshape([-1 if axis == position else 1 for axis in range(len(dims))])
    return level


def scatter_about(rng, dims, deviation, bound, pieces=(), kind=jnp.bfloat16):
    entries = deviation * jax.random.normal(rng, dims, jnp.float32)
    if pieces:
        entries = entries * shard_levels(rng, dims, pieces, -0.22, 0.18)
    return jnp.clip(entries, -bound, bound).astype(kind)


def setup_inputs(seed: int = 0) -> dict:
    seeds = jax.random.split(jax.random.key(seed), 6)
    probes = draw_probes(jax.random.fold_in(seeds[5], 71), 0)
    sensitivity = scatter_about(seeds[1], (GAUSS, NPE, ELEMS), 0.35, 2.1, ((2, 32),), jnp.float32)
    obs_weight = jnp.clip(jnp.exp(math.log(4.0) - 2.0794415 * jax.random.uniform(seeds[2], (GAUSS, ELEMS), jnp.float32) ** shard_levels(seeds[2], (GAUSS, ELEMS), ((1, 32),), -0.2, 0.2)), 0.5, 4.0)
    prior_weight = jnp.clip(jnp.exp(math.log(2.0) - 2.3025851 * jax.random.uniform(seeds[3], (NODES,), jnp.float32) ** shard_levels(seeds[3], (NODES,), ((0, 32),), -0.2, 0.2)), 0.2, 2.0)
    connectivity = draw_connectivity(jax.random.fold_in(seeds[5], 71), 0)
    return {"probes": probes, "sensitivity": sensitivity, "obs_weight": obs_weight, "prior_weight": prior_weight, "connectivity": connectivity}


highest = lax.Precision.HIGHEST

def reference(probes, sensitivity, obs_weight, prior_weight, connectivity):
    element = jnp.arange(ELEMS, dtype=jnp.int32)
    offsets = (element // ED * ND - HALO).astype(jnp.int32)
    node = (connectivity + offsets[None, :]).astype(jnp.int32)

    def apply_column(column):
        gathered = column[node]
        observed = jnp.einsum('gce,ce->ge', sensitivity, gathered, precision=highest) * obs_weight
        pulled = jnp.einsum('gce,ge->ce', sensitivity, observed, precision=highest)
        summed = jnp.zeros((NODES,), jnp.float32).at[node].add(pulled)
        return summed + prior_weight * column
    images = lax.map(apply_column, probes)
    gram_first = jnp.dot(images.astype(jnp.float32), images.T.astype(jnp.float32), precision=highest, preferred_element_type=jnp.float32)
    lower_first = jnp.linalg.cholesky(gram_first)
    basis_first = lax.linalg.triangular_solve(lower_first, images, left_side=True, lower=True)
    gram_second = jnp.dot(basis_first.astype(jnp.float32), basis_first.T.astype(jnp.float32), precision=highest, preferred_element_type=jnp.float32)
    lower_second = jnp.linalg.cholesky(gram_second)
    basis = lax.linalg.triangular_solve(lower_second, basis_first, left_side=True, lower=True)
    scale = jnp.sqrt(jnp.float32(NODES))
    factor = jnp.dot(lower_first.astype(jnp.float32), lower_second.astype(jnp.float32), precision=highest, preferred_element_type=jnp.float32).T
    return (basis * scale, factor / scale)
```

```python
import math

import jax
import jax.numpy as jnp
from jax import lax
from jax.experimental import pallas as pl
from jax.experimental.pallas import tpu as pltpu
from jax.sharding import PartitionSpec as P

HALO = 128
LANES = 128
WIDE = 256

highest = lax.Precision.HIGHEST


def shifted(block, axis, distance):
    devices = range(lax.axis_size(axis))
    route = [(i - distance, i) for i in devices if i - distance in devices]
    return lax.ppermute(block, axis, route)


def element_kernel(
    low_ref, probes_ref, high_ref, connectivity_ref, sensitivity_ref, weight_ref, prior_ref,
    images_ref, lower_ref, upper_ref, left_ref, right_ref, total_ref,
):
    probe_count, node_count = probes_ref.shape
    corner_count, element_count = connectivity_ref.shape
    gauss_count = sensitivity_ref.shape[0]
    tiles = node_count // LANES + 2
    blocks = tiles * LANES // WIDE
    rows = total_ref.shape[0]

    def tile(k):
        if k == 0:
            return low_ref[...]
        if k == tiles - 1:
            return high_ref[...]
        return probes_ref[:, (k - 1) * LANES : k * LANES]

    total_ref[...] = jnp.zeros_like(total_ref)

    def chunk(step, carry):
        columns = pl.ds(pl.multiple_of(step * LANES, LANES), LANES)
        gathered = []
        nodes = []
        for corner in range(corner_count):
            node = jnp.broadcast_to(
                connectivity_ref[corner : corner + 1, columns], (probe_count, LANES)
            )
            nodes.append(node)
            lane = node & (LANES - 1)
            place = lax.shift_right_logical(node, 7)
            value = jnp.zeros((probe_count, LANES), jnp.float32)
            for k in range(tiles):
                picked = jnp.take_along_axis(tile(k), lane, axis=1, mode="promise_in_bounds")
                value = jnp.where(place == k, picked, value)
            gathered.append(value)
        observed = []
        for gauss in range(gauss_count):
            value = gathered[0] * sensitivity_ref[gauss, 0:1, columns]
            for corner in range(1, corner_count):
                value = value + gathered[corner] * sensitivity_ref[gauss, corner : corner + 1, columns]
            observed.append(value * weight_ref[gauss : gauss + 1, columns])
        for corner in range(corner_count):
            value = observed[0] * sensitivity_ref[0, corner : corner + 1, columns]
            for gauss in range(1, gauss_count):
                value = value + observed[gauss] * sensitivity_ref[gauss, corner : corner + 1, columns]
            first = value.astype(jnp.bfloat16).astype(jnp.float32)
            rest = value - first
            second = rest.astype(jnp.bfloat16).astype(jnp.float32)
            third = rest - second
            node = nodes[corner]
            place = lax.shift_right_logical(node, 8)
            zero = jnp.zeros_like(value)
            pieces = []
            for k in range(blocks):
                here = place == k
                for piece in (first, second, third):
                    pieces.append(jnp.where(here, piece, zero))
            while len(pieces) * probe_count < rows:
                pieces.append(zero)
            span = slice(corner * LANES, (corner + 1) * LANES)
            left_ref[:, span] = jnp.concatenate(pieces, axis=0).astype(jnp.bfloat16)
            lane = jnp.broadcast_to(node[0:1, :] & (WIDE - 1), (WIDE, LANES))
            row = lax.broadcasted_iota(jnp.int32, (WIDE, LANES), 0)
            right_ref[:, span] = jnp.where(row == lane, 1.0, 0.0).astype(jnp.bfloat16)
        total_ref[...] += lax.dot_general(
            left_ref[...], right_ref[...], (((1,), (1,)), ((), ())),
            preferred_element_type=jnp.float32,
        )
        return carry

    lax.fori_loop(0, element_count // LANES, chunk, 0)

    for block in range(blocks):
        at = block * 3 * probe_count
        value = total_ref[at + 2 * probe_count : at + 3 * probe_count, :]
        value = value + total_ref[at + probe_count : at + 2 * probe_count, :]
        value = value + total_ref[at : at + probe_count, :]
        for half in range(WIDE // LANES):
            k = block * (WIDE // LANES) + half
            part = value[:, half * LANES : (half + 1) * LANES]
            if k == 0:
                lower_ref[...] = part
            elif k == tiles - 1:
                upper_ref[...] = part
            else:
                span = slice((k - 1) * LANES, k * LANES)
                images_ref[:, span] = part + prior_ref[:, span] * probes_ref[:, span]


def element_images(low, probes, high, connectivity, sensitivity, obs_weight, prior_weight):
    probe_count, node_count = probes.shape
    corner_count = connectivity.shape[0]
    blocks = (node_count + 2 * HALO) // WIDE
    rows = -(-blocks * 3 * probe_count // 16) * 16
    vmem = pl.BlockSpec(memory_space=pltpu.VMEM)
    rim = jax.ShapeDtypeStruct((probe_count, HALO), jnp.float32)
    return pl.pallas_call(
        element_kernel,
        out_shape=(jax.ShapeDtypeStruct(probes.shape, jnp.float32), rim, rim),
        in_specs=[vmem] * 7,
        out_specs=(vmem, vmem, vmem),
        scratch_shapes=[
            pltpu.VMEM((rows, corner_count * LANES), jnp.bfloat16),
            pltpu.VMEM((WIDE, corner_count * LANES), jnp.bfloat16),
            pltpu.VMEM((rows, WIDE), jnp.float32),
        ],
        name="element_images",
    )(low, probes, high, connectivity, sensitivity, obs_weight, prior_weight.reshape(1, -1))


def gram_over_space(partial_value):
    return lax.psum(partial_value, "space")


def orthonormal(rows, reduce_gram):
    gram_first = reduce_gram(
        jnp.dot(rows, rows.T, precision=highest, preferred_element_type=jnp.float32)
    )
    lower_first = jnp.linalg.cholesky(gram_first)
    basis_first = lax.linalg.triangular_solve(lower_first, rows, left_side=True, lower=True)
    gram_second = reduce_gram(
        jnp.dot(basis_first, basis_first.T, precision=highest, preferred_element_type=jnp.float32)
    )
    lower_second = jnp.linalg.cholesky(gram_second)
    basis = lax.linalg.triangular_solve(lower_second, basis_first, left_side=True, lower=True)
    factor = jnp.dot(
        lower_first, lower_second, precision=highest, preferred_element_type=jnp.float32
    ).T
    return (basis, factor)


def on_device(probes, sensitivity, obs_weight, prior_weight, connectivity):
    node_count = probes.shape[1]
    probe_count = probes.shape[0]
    low = shifted(probes[:, node_count - HALO :], "space", 1)
    high = shifted(probes[:, :HALO], "space", -1)
    images, lower, upper = element_images(
        low, probes, high, connectivity, sensitivity, obs_weight, prior_weight
    )
    lower_rim = shifted(lower, "space", -1)
    upper_rim = shifted(upper, "space", 1)
    images = images.at[:, node_count - HALO :].add(lower_rim)
    images = images.at[:, :HALO].add(upper_rim)
    scale = math.sqrt(float(node_count * lax.axis_size("space")))
    whole = lax.all_gather(images, "probe", axis=0, tiled=True)
    basis, factor = orthonormal(whole, gram_over_space)
    basis = lax.dynamic_slice_in_dim(basis, lax.axis_index("probe") * probe_count, probe_count, 0)
    return (basis * scale, factor / scale)


def solution(mesh):
    return jax.shard_map(
        on_device,
        mesh=mesh,
        in_specs=(
            P("probe", "space"),
            P(None, None, "space"),
            P(None, "space"),
            P("space"),
            P(None, "space"),
        ),
        out_specs=(P("probe", "space"), P()),
        check_vma=False,
    )
```

```python
import functools
import math

import jax
import jax.numpy as jnp
from jax import lax
from jax.experimental import pallas as pl
from jax.experimental.pallas import tpu as pltpu
from jax.sharding import PartitionSpec as P

HALO = 128
LANES = 128
WIDE = 256
CORES = 2

highest = lax.Precision.HIGHEST


def shifted(block, axis, distance):
    devices = range(lax.axis_size(axis))
    route = [(i - distance, i) for i in devices if i - distance in devices]
    return lax.ppermute(block, axis, route)


def element_kernel(
    low_ref, probes_ref, high_ref, connectivity_ref, sensitivity_ref, weight_ref, prior_ref,
    images_ref, lower_ref, upper_ref, left_ref, right_ref, total_ref,
):
    probe_count, node_count = probes_ref.shape
    corner_count, element_count = connectivity_ref.shape
    gauss_count = sensitivity_ref.shape[0]
    tiles = node_count // LANES + 2
    blocks = tiles * LANES // WIDE
    rows = total_ref.shape[0]

    def tile(k):
        if k == 0:
            return low_ref[...]
        if k == tiles - 1:
            return high_ref[...]
        return probes_ref[:, (k - 1) * LANES : k * LANES]

    total_ref[...] = jnp.zeros_like(total_ref)

    def chunk(step, carry):
        columns = pl.ds(pl.multiple_of(step * LANES, LANES), LANES)
        gathered = []
        nodes = []
        for corner in range(corner_count):
            node = jnp.broadcast_to(
                connectivity_ref[corner : corner + 1, columns], (probe_count, LANES)
            )
            nodes.append(node)
            lane = node & (LANES - 1)
            place = lax.shift_right_logical(node, 7)
            value = jnp.zeros((probe_count, LANES), jnp.float32)
            for k in range(tiles):
                picked = jnp.take_along_axis(tile(k), lane, axis=1, mode="promise_in_bounds")
                value = jnp.where(place == k, picked, value)
            gathered.append(value)
        observed = []
        for gauss in range(gauss_count):
            value = gathered[0] * sensitivity_ref[gauss, 0:1, columns]
            for corner in range(1, corner_count):
                value = value + gathered[corner] * sensitivity_ref[gauss, corner : corner + 1, columns]
            observed.append(value * weight_ref[gauss : gauss + 1, columns])
        for corner in range(corner_count):
            value = observed[0] * sensitivity_ref[0, corner : corner + 1, columns]
            for gauss in range(1, gauss_count):
                value = value + observed[gauss] * sensitivity_ref[gauss, corner : corner + 1, columns]
            first = value.astype(jnp.bfloat16).astype(jnp.float32)
            rest = value - first
            second = rest.astype(jnp.bfloat16).astype(jnp.float32)
            third = rest - second
            node = nodes[corner]
            place = lax.shift_right_logical(node, 8)
            zero = jnp.zeros_like(value)
            pieces = []
            for k in range(blocks):
                here = place == k
                for piece in (first, second, third):
                    pieces.append(jnp.where(here, piece, zero))
            while len(pieces) * probe_count < rows:
                pieces.append(zero)
            span = slice(corner * LANES, (corner + 1) * LANES)
            left_ref[:, span] = jnp.concatenate(pieces, axis=0).astype(jnp.bfloat16)
            lane = jnp.broadcast_to(node[0:1, :] & (WIDE - 1), (WIDE, LANES))
            row = lax.broadcasted_iota(jnp.int32, (WIDE, LANES), 0)
            right_ref[:, span] = jnp.where(row == lane, 1.0, 0.0).astype(jnp.bfloat16)
        total_ref[...] += lax.dot_general(
            left_ref[...], right_ref[...], (((1,), (1,)), ((), ())),
            preferred_element_type=jnp.float32,
        )
        return carry

    lax.fori_loop(0, element_count // LANES, chunk, 0)

    for block in range(blocks):
        at = block * 3 * probe_count
        value = total_ref[at + 2 * probe_count : at + 3 * probe_count, :]
        value = value + total_ref[at + probe_count : at + 2 * probe_count, :]
        value = value + total_ref[at : at + probe_count, :]
        for half in range(WIDE // LANES):
            k = block * (WIDE // LANES) + half
            part = value[:, half * LANES : (half + 1) * LANES]
            if k == 0:
                lower_ref[...] = part
            elif k == tiles - 1:
                upper_ref[...] = part
            else:
                span = slice((k - 1) * LANES, k * LANES)
                images_ref[:, span] = part + prior_ref[:, span] * probes_ref[:, span]


def element_images(low, probes, high, connectivity, sensitivity, obs_weight, prior_weight):
    probe_count, node_count = probes.shape
    corner_count = connectivity.shape[0]
    blocks = (node_count + 2 * HALO) // WIDE
    rows = -(-blocks * 3 * probe_count // 16) * 16
    vmem = pl.BlockSpec(memory_space=pltpu.VMEM)
    rim = jax.ShapeDtypeStruct((probe_count, HALO), jnp.float32)
    return pl.pallas_call(
        element_kernel,
        out_shape=(jax.ShapeDtypeStruct(probes.shape, jnp.float32), rim, rim),
        in_specs=[vmem] * 7,
        out_specs=(vmem, vmem, vmem),
        scratch_shapes=[
            pltpu.VMEM((rows, corner_count * LANES), jnp.bfloat16),
            pltpu.VMEM((WIDE, corner_count * LANES), jnp.bfloat16),
            pltpu.VMEM((rows, WIDE), jnp.float32),
        ],
        name="element_images",
    )(low, probes, high, connectivity, sensitivity, obs_weight, prior_weight.reshape(1, -1))


SUBLANES = 8
SLICE = 2.0**-8
PROBE_SLICES = 4
GRAM_SLICES = 5
INVERSE_SLICES = 4
FIRST_SLICES = 5


def power_of_two(value):
    return jnp.exp(value * math.log(2.0)).astype(jnp.bfloat16).astype(jnp.float32)


def bound_of(magnitude):
    return power_of_two(jnp.floor(jnp.log(magnitude) * (1.0 / math.log(2.0))) + 1.0)


def sliced(value, bound, count, late=None, late_at=0):
    sigma = bound * (1.5 * 2.0**16)
    slices = []
    for k in range(count):
        if late is not None and k == late_at:
            value = value + late
        piece = (value + sigma) - sigma
        slices.append(piece)
        value = value - piece
        sigma = sigma * SLICE
    return slices


def two_sum(a, b):
    total = a + b
    part = total - a
    return total, (a - (total - part)) + (b - part)


def added(left, right):
    total, error = two_sum(left[0], right[0])
    error = error + (left[1] + right[1])
    high = total + error
    return high, error - (high - total)


def add_levels(blocks, rows, columns, levels):
    high = low = None
    for level in range(levels):
        part = None
        for a in range(rows):
            b = level - a
            if 0 <= b < columns:
                part = blocks(a, b) if part is None else part + blocks(a, b)
        if high is None:
            high, low = part, jnp.zeros_like(part)
        else:
            high, error = two_sum(high, part)
            low = low + error
    total = high + low
    return total, low - (total - high)


def block_reader(products, size):
    return lambda a, b: products[a * size : (a + 1) * size, b * size : (b + 1) * size]


def gram_kernel(rows_ref, pair_ref):
    rows = rows_ref[...]
    size = rows.shape[0]
    bound = bound_of(jnp.max(jnp.abs(rows), axis=1, keepdims=True))
    stacked = jnp.concatenate(sliced(rows, bound, PROBE_SLICES), axis=0).astype(jnp.bfloat16)
    products = lax.dot_general(
        stacked, stacked, (((1,), (1,)), ((), ())), preferred_element_type=jnp.float32
    )
    high, low = add_levels(block_reader(products, size), PROBE_SLICES, PROBE_SLICES, 5)
    parts, double, _ = pair_ref.shape
    count = double // 2
    for part in range(parts):
        pair_ref[part, :count, :] = high[part * count : (part + 1) * count, :]
        pair_ref[part, count:, :] = low[part * count : (part + 1) * count, :]


def pairs_added(pairs):
    while len(pairs) > 1:
        joined = [added(a, b) for a, b in zip(pairs[::2], pairs[1::2])]
        pairs = joined + pairs[len(pairs) // 2 * 2 :]
    return pairs[0]


def halves(block):
    count = block.shape[0] // 2
    return block[:count, :], block[count:, :]


def sum_kernel(parts_ref, total_ref):
    high, low = pairs_added([halves(parts_ref[k]) for k in range(parts_ref.shape[0])])
    total_ref[...] = jnp.concatenate([high, low], axis=0)


def spread_kernel(own_ref, other_ref, copies_ref):
    high, low = added(halves(own_ref[...]), halves(other_ref[...]))
    total = jnp.concatenate([high, low], axis=0)
    for k in range(copies_ref.shape[0]):
        copies_ref[k] = total


def sum_spread_kernel(parts_ref, copies_ref):
    high, low = pairs_added([halves(parts_ref[k]) for k in range(parts_ref.shape[0])])
    total = jnp.concatenate([high, low], axis=0)
    for k in range(copies_ref.shape[0]):
        copies_ref[k] = total


def triangles(gram):
    size = gram.shape[0]
    tiles = [gram[k * SUBLANES : (k + 1) * SUBLANES, :] for k in range(size // SUBLANES)]
    pivots = [jnp.ones((SUBLANES, size), jnp.float32) for _ in tiles]
    lane = lax.broadcasted_iota(jnp.int32, (SUBLANES, size), 1)
    sub = lax.broadcasted_iota(jnp.int32, (SUBLANES, size), 0)
    for j in range(size):
        own, at = divmod(j, SUBLANES)
        here = lane == j
        row = jnp.broadcast_to(tiles[own][at : at + 1, :], (SUBLANES, size))
        pivot = jnp.broadcast_to(row[:, j : j + 1], (SUBLANES, size))
        scaled = jnp.where(here, 1.0, row) * (1.0 / pivot)
        for k in range(own, len(tiles)):
            column = jnp.broadcast_to(tiles[k][:, j : j + 1], (SUBLANES, size))
            clear = here
            if k == own:
                column = jnp.where(sub > at, column, 0.0)
                clear = here & (sub > at)
                pivots[k] = jnp.where(sub == at, pivot, pivots[k])
            tiles[k] = jnp.where(clear, 0.0, tiles[k]) - column * scaled
    upper, inverse = [], []
    for k, tile in enumerate(tiles):
        root = lax.rsqrt(pivots[k])
        root = root * (1.5 - 0.5 * pivots[k] * root * root)
        row = sub + k * SUBLANES
        upper.append(jnp.where(lane >= row, tile * root, 0.0))
        inverse.append(jnp.where(lane > row, 0.0, jnp.where(lane == row, root, tile * root)))
    return jnp.concatenate(upper, axis=0), jnp.concatenate(inverse, axis=0)


def exact(a, b):
    return jnp.dot(a, b, precision=highest, preferred_element_type=jnp.float32)


def basis_kernel(scale, pair_ref, rows_ref, basis_ref, factor_ref):
    parts, double, size = pair_ref.shape
    count = double // 2
    high = jnp.concatenate([pair_ref[k, :count, :] for k in range(parts)], axis=0)
    low = jnp.concatenate([pair_ref[k, count:, :] for k in range(parts)], axis=0)
    lane = lax.broadcasted_iota(jnp.int32, (size, size), 1)
    sub = lax.broadcasted_iota(jnp.int32, (size, size), 0)
    diagonal = jnp.where(lane == sub, high, 0.0)
    down = jnp.floor(jnp.log(jnp.max(diagonal, axis=1, keepdims=True)) * (0.5 / math.log(2.0)))
    across = jnp.floor(jnp.log(jnp.max(diagonal, axis=0, keepdims=True)) * (0.5 / math.log(2.0)))
    shrink = power_of_two(-down)
    shrink_across = power_of_two(-across)
    four = jnp.where(shrink > 0.0, 4.0, 8.0)
    high = high * shrink * shrink_across
    low = low * shrink * shrink_across

    upper_first, inverse_first = triangles(high)

    gram_slices = sliced(high, four, GRAM_SLICES, late=low, late_at=3)
    bound = bound_of(jnp.max(jnp.abs(inverse_first), axis=1, keepdims=True))
    inverse_slices = sliced(inverse_first, bound, INVERSE_SLICES)
    gram_stack = jnp.concatenate(gram_slices, axis=0).astype(jnp.bfloat16)
    inverse_stack = jnp.concatenate(inverse_slices, axis=0).astype(jnp.bfloat16)
    products = lax.dot_general(
        gram_stack, inverse_stack, (((1,), (1,)), ((), ())), preferred_element_type=jnp.float32
    )
    lower_high, lower_low = add_levels(
        block_reader(products, size), GRAM_SLICES, INVERSE_SLICES, 6
    )
    lower_slices = sliced(lower_high, four, FIRST_SLICES, late=lower_low, late_at=3)
    lower_stack = jnp.concatenate(lower_slices, axis=1).astype(jnp.bfloat16)
    products = jnp.dot(inverse_stack, lower_stack, preferred_element_type=jnp.float32)
    gram_second, rest = add_levels(
        block_reader(products, size), INVERSE_SLICES, FIRST_SLICES, 5
    )
    gram_second = gram_second + rest

    upper_second, inverse_second = triangles(gram_second)
    basis_first = exact(inverse_first, rows_ref[...] * shrink)
    basis = exact(inverse_second, basis_first)
    basis_ref[...] = basis * scale
    factor = exact(upper_second, upper_first)
    factor_ref[...] = factor * (power_of_two(across) * (1.0 / scale))


def in_vmem(kernel, name, out_shape, *operands):
    vmem = pl.BlockSpec(memory_space=pltpu.VMEM)
    single = not isinstance(out_shape, tuple)
    return pl.pallas_call(
        kernel,
        out_shape=out_shape,
        in_specs=[vmem] * len(operands),
        out_specs=vmem if single else tuple(vmem for _ in out_shape),
        name=name,
    )(*operands)


def orthonormal(rows, scale):
    size = rows.shape[0]
    parts = lax.axis_size("probe")
    count = 2 * size // parts
    places = lax.axis_size("space")
    pair = jax.ShapeDtypeStruct((parts, count, size), jnp.float32)
    one = jax.ShapeDtypeStruct((count, size), jnp.float32)
    levels = places // CORES
    copies = jax.ShapeDtypeStruct((levels, count, size), jnp.float32)
    gram = in_vmem(gram_kernel, "gram", pair, rows)
    gram = lax.all_to_all(gram, "probe", 0, 0, tiled=True)
    own = in_vmem(sum_kernel, "probe_sum", one, gram)
    other = lax.ppermute(own, "space", [(k, k ^ 1) for k in range(places)])
    spread = in_vmem(spread_kernel, "core_sum", copies, own, other)
    groups = [[core + CORES * k for k in range(levels)] for core in range(CORES)]
    spread = lax.all_to_all(spread, "space", 0, 0, tiled=True, axis_index_groups=groups)
    whole = in_vmem(sum_spread_kernel, "space_sum", pair, spread)
    whole = lax.all_to_all(whole, "probe", 0, 0, tiled=True)
    return in_vmem(
        functools.partial(basis_kernel, scale), "basis",
        (
            jax.ShapeDtypeStruct(rows.shape, jnp.float32),
            jax.ShapeDtypeStruct((size, size), jnp.float32),
        ),
        whole, rows,
    )


def on_device(probes, sensitivity, obs_weight, prior_weight, connectivity):
    node_count = probes.shape[1]
    low = shifted(probes[:, node_count - HALO :], "space", 1)
    high = shifted(probes[:, :HALO], "space", -1)
    images, lower, upper = element_images(
        low, probes, high, connectivity, sensitivity, obs_weight, prior_weight
    )
    lower_rim = shifted(lower, "space", -1)
    upper_rim = shifted(upper, "space", 1)
    images = images.at[:, node_count - HALO :].add(lower_rim)
    images = images.at[:, :HALO].add(upper_rim)
    scale = math.sqrt(float(node_count * lax.axis_size("space")))
    rows = lax.all_to_all(images, "probe", 1, 0, tiled=True)
    basis, factor = orthonormal(rows, scale)
    return lax.all_to_all(basis, "probe", 0, 1, tiled=True), factor


def solution(mesh):
    return jax.shard_map(
        on_device,
        mesh=mesh,
        in_specs=(
            P("probe", "space"),
            P(None, None, "space"),
            P(None, "space"),
            P("space"),
            P(None, "space"),
        ),
        out_specs=(P("probe", "space"), P()),
        check_vma=False,
    )
```

```python
import functools
import math

import jax
import jax.numpy as jnp
from jax import lax
from jax.experimental import pallas as pl
from jax.experimental.pallas import tpu as pltpu
from jax.sharding import PartitionSpec as P

HALO = 128
LANES = 128
WIDE = 256
CORES = 2

highest = lax.Precision.HIGHEST


def shifted(block, axis, distance):
    devices = range(lax.axis_size(axis))
    route = [(i - distance, i) for i in devices if i - distance in devices]
    return lax.ppermute(block, axis, route)


def element_kernel(
    low_ref, probes_ref, high_ref, connectivity_ref, sensitivity_ref, weight_ref, prior_ref,
    images_ref, lower_ref, upper_ref, left_ref, right_ref, total_ref,
):
    probe_count, node_count = probes_ref.shape
    corner_count, element_count = connectivity_ref.shape
    gauss_count = sensitivity_ref.shape[0]
    tiles = node_count // LANES + 2
    blocks = tiles * LANES // WIDE
    rows = total_ref.shape[0]

    def tile(k):
        if k == 0:
            return low_ref[...]
        if k == tiles - 1:
            return high_ref[...]
        return probes_ref[:, (k - 1) * LANES : k * LANES]

    total_ref[...] = jnp.zeros_like(total_ref)

    def chunk(step, carry):
        columns = pl.ds(pl.multiple_of(step * LANES, LANES), LANES)
        gathered = []
        nodes = []
        for corner in range(corner_count):
            node = jnp.broadcast_to(
                connectivity_ref[corner : corner + 1, columns], (probe_count, LANES)
            )
            nodes.append(node)
            lane = node & (LANES - 1)
            place = lax.shift_right_logical(node, 7)
            value = jnp.zeros((probe_count, LANES), jnp.float32)
            for k in range(tiles):
                picked = jnp.take_along_axis(tile(k), lane, axis=1, mode="promise_in_bounds")
                value = jnp.where(place == k, picked, value)
            gathered.append(value)
        observed = []
        for gauss in range(gauss_count):
            value = gathered[0] * sensitivity_ref[gauss, 0:1, columns]
            for corner in range(1, corner_count):
                value = value + gathered[corner] * sensitivity_ref[gauss, corner : corner + 1, columns]
            observed.append(value * weight_ref[gauss : gauss + 1, columns])
        for corner in range(corner_count):
            value = observed[0] * sensitivity_ref[0, corner : corner + 1, columns]
            for gauss in range(1, gauss_count):
                value = value + observed[gauss] * sensitivity_ref[gauss, corner : corner + 1, columns]
            first = value.astype(jnp.bfloat16).astype(jnp.float32)
            rest = value - first
            second = rest.astype(jnp.bfloat16).astype(jnp.float32)
            third = rest - second
            node = nodes[corner]
            place = lax.shift_right_logical(node, 8)
            zero = jnp.zeros_like(value)
            pieces = []
            for k in range(blocks):
                here = place == k
                for piece in (first, second, third):
                    pieces.append(jnp.where(here, piece, zero))
            while len(pieces) * probe_count < rows:
                pieces.append(zero)
            span = slice(corner * LANES, (corner + 1) * LANES)
            left_ref[:, span] = jnp.concatenate(pieces, axis=0).astype(jnp.bfloat16)
            lane = jnp.broadcast_to(node[0:1, :] & (WIDE - 1), (WIDE, LANES))
            row = lax.broadcasted_iota(jnp.int32, (WIDE, LANES), 0)
            right_ref[:, span] = jnp.where(row == lane, 1.0, 0.0).astype(jnp.bfloat16)
        total_ref[...] += lax.dot_general(
            left_ref[...], right_ref[...], (((1,), (1,)), ((), ())),
            preferred_element_type=jnp.float32,
        )
        return carry

    lax.fori_loop(0, element_count // LANES, chunk, 0)

    for block in range(blocks):
        at = block * 3 * probe_count
        value = total_ref[at + 2 * probe_count : at + 3 * probe_count, :]
        value = value + total_ref[at + probe_count : at + 2 * probe_count, :]
        value = value + total_ref[at : at + probe_count, :]
        for half in range(WIDE // LANES):
            k = block * (WIDE // LANES) + half
            part = value[:, half * LANES : (half + 1) * LANES]
            if k == 0:
                lower_ref[...] = part
            elif k == tiles - 1:
                upper_ref[...] = part
            else:
                span = slice((k - 1) * LANES, k * LANES)
                images_ref[:, span] = part + prior_ref[:, span] * probes_ref[:, span]


def element_images(low, probes, high, connectivity, sensitivity, obs_weight, prior_weight):
    probe_count, node_count = probes.shape
    corner_count = connectivity.shape[0]
    blocks = (node_count + 2 * HALO) // WIDE
    rows = -(-blocks * 3 * probe_count // 16) * 16
    vmem = pl.BlockSpec(memory_space=pltpu.VMEM)
    rim = jax.ShapeDtypeStruct((probe_count, HALO), jnp.float32)
    return pl.pallas_call(
        element_kernel,
        out_shape=(jax.ShapeDtypeStruct(probes.shape, jnp.float32), rim, rim),
        in_specs=[vmem] * 7,
        out_specs=(vmem, vmem, vmem),
        scratch_shapes=[
            pltpu.VMEM((rows, corner_count * LANES), jnp.bfloat16),
            pltpu.VMEM((WIDE, corner_count * LANES), jnp.bfloat16),
            pltpu.VMEM((rows, WIDE), jnp.float32),
        ],
        name="element_images",
    )(low, probes, high, connectivity, sensitivity, obs_weight, prior_weight.reshape(1, -1))


SUBLANES = 8
GROUP = 2
SLICE = 2.0**-8
PROBE_SLICES = 4
GRAM_SLICES = 5
INVERSE_SLICES = 4
FIRST_SLICES = 5


def power_of_two(value):
    return jnp.exp(value * math.log(2.0)).astype(jnp.bfloat16).astype(jnp.float32)


def bound_of(magnitude):
    return power_of_two(jnp.floor(jnp.log(magnitude) * (1.0 / math.log(2.0))) + 1.0)


def sliced(value, bound, count, late=None, late_at=0):
    sigma = bound * (1.5 * 2.0**16)
    slices = []
    for k in range(count):
        if late is not None and k == late_at:
            value = value + late
        piece = (value + sigma) - sigma
        slices.append(piece)
        value = value - piece
        sigma = sigma * SLICE
    return slices


def two_sum(a, b):
    total = a + b
    part = total - a
    return total, (a - (total - part)) + (b - part)


def added(left, right):
    total, error = two_sum(left[0], right[0])
    error = error + (left[1] + right[1])
    high = total + error
    return high, error - (high - total)


def add_levels(blocks, rows, columns, levels):
    high = low = None
    for level in range(levels):
        part = None
        for a in range(rows):
            b = level - a
            if 0 <= b < columns:
                part = blocks(a, b) if part is None else part + blocks(a, b)
        if high is None:
            high, low = part, jnp.zeros_like(part)
        else:
            high, error = two_sum(high, part)
            low = low + error
    total = high + low
    return total, low - (total - high)


def block_reader(products, size):
    return lambda a, b: products[a * size : (a + 1) * size, b * size : (b + 1) * size]


def gram_kernel(rows_ref, pair_ref):
    rows = rows_ref[...]
    size = rows.shape[0]
    bound = bound_of(jnp.max(jnp.abs(rows), axis=1, keepdims=True))
    stacked = jnp.concatenate(sliced(rows, bound, PROBE_SLICES), axis=0).astype(jnp.bfloat16)
    products = lax.dot_general(
        stacked, stacked, (((1,), (1,)), ((), ())), preferred_element_type=jnp.float32
    )
    high, low = add_levels(block_reader(products, size), PROBE_SLICES, PROBE_SLICES, 5)
    parts, double, _ = pair_ref.shape
    count = double // 2
    for part in range(parts):
        pair_ref[part, :count, :] = high[part * count : (part + 1) * count, :]
        pair_ref[part, count:, :] = low[part * count : (part + 1) * count, :]


def pairs_added(pairs):
    while len(pairs) > 1:
        joined = [added(a, b) for a, b in zip(pairs[::2], pairs[1::2])]
        pairs = joined + pairs[len(pairs) // 2 * 2 :]
    return pairs[0]


def halves(block):
    count = block.shape[0] // 2
    return block[:count, :], block[count:, :]


def sum_kernel(parts_ref, total_ref):
    high, low = pairs_added([halves(parts_ref[k]) for k in range(parts_ref.shape[0])])
    total_ref[...] = jnp.concatenate([high, low], axis=0)


def spread_kernel(own_ref, other_ref, copies_ref):
    high, low = added(halves(own_ref[...]), halves(other_ref[...]))
    total = jnp.concatenate([high, low], axis=0)
    for k in range(copies_ref.shape[0]):
        copies_ref[k] = total


def sum_spread_kernel(parts_ref, copies_ref):
    high, low = pairs_added([halves(parts_ref[k]) for k in range(parts_ref.shape[0])])
    total = jnp.concatenate([high, low], axis=0)
    for k in range(copies_ref.shape[0]):
        copies_ref[k] = total


def eliminate_group(tiles, pivots, at):
    shape = tiles[0].shape
    lane = lax.broadcasted_iota(jnp.int32, shape, 1)
    sub = lax.broadcasted_iota(jnp.int32, shape, 0)
    chosen = range(GROUP)
    columns = [[jnp.broadcast_to(tile[:, at + r : at + r + 1], shape) for r in chosen] for tile in tiles]
    entry = [
        [jnp.broadcast_to(columns[0][c][at + r : at + r + 1, :], shape) for c in chosen] for r in chosen
    ]
    rows = [jnp.broadcast_to(tiles[0][at + r : at + r + 1, :], shape) for r in chosen]
    factor = [[None] * GROUP for _ in chosen]
    scaled = []
    for s in chosen:
        over = 1.0 / entry[s][s]
        here = lane == at + s
        with_one = jnp.where(here, 1.0, rows[s])
        for r in range(s + 1, GROUP):
            factor[s][r] = entry[s][r] * over
            for c in range(r, GROUP):
                entry[r][c] = entry[r][c] - factor[s][r] * entry[s][c]
            rows[r] = jnp.where(here, 0.0, rows[r]) - factor[s][r] * with_one
        later = (lane > at + s) & (lane < at + GROUP)
        scaled.append(jnp.where(later, 0.0, with_one) * over)
    inside = (lane >= at) & (lane < at + GROUP)
    done = []
    for k, tile in enumerate(tiles):
        clear = inside
        if k == 0:
            below = sub >= at + GROUP
            clear = inside & below
        new = jnp.where(clear, 0.0, tile)
        own = list(columns[k])
        for s in chosen:
            for r in range(s + 1, GROUP):
                own[r] = own[r] - own[s] * factor[s][r]
        for s in chosen:
            value = jnp.where(below, own[s], 0.0) if k == 0 else own[s]
            new = new - value * scaled[s]
        if k == 0:
            for s in chosen:
                new = jnp.where(sub == at + s, rows[s], new)
                pivots = jnp.where(sub == at + s, entry[s][s], pivots)
        done.append(new)
    return done, pivots


def triangles(gram, tile_ref, pivot_ref):
    size = gram.shape[0]
    count = size // SUBLANES
    tiles = [gram[k * SUBLANES : (k + 1) * SUBLANES, :] for k in range(count)]

    def block(step, tiles):
        tiles = list(tiles)
        pivots = jnp.ones((SUBLANES, size), jnp.float32)
        for at in range(0, SUBLANES, GROUP):
            tiles, pivots = eliminate_group(tiles, pivots, at)
        place = pl.ds(pl.multiple_of(step * SUBLANES, SUBLANES), SUBLANES)
        tile_ref[place, :] = pltpu.roll(tiles[0], step * SUBLANES, 1)
        pivot_ref[place, :] = pivots
        tiles = [pltpu.roll(tile, size - SUBLANES, 1) for tile in tiles]
        return tuple(tiles[1:] + tiles[:1])

    half = count // 2
    tiles = lax.fori_loop(0, half, block, tuple(tiles))
    lax.fori_loop(half, count, block, tuple(tiles[:half]))
    tile, pivot = tile_ref[...], pivot_ref[...]
    lane = lax.broadcasted_iota(jnp.int32, tile.shape, 1)
    row = lax.broadcasted_iota(jnp.int32, tile.shape, 0)
    root = lax.rsqrt(pivot)
    root = root * (1.5 - 0.5 * pivot * root * root)
    scaled = tile * root
    upper = jnp.where(lane > row, scaled, jnp.where(lane == row, pivot * root, 0.0))
    inverse = jnp.where(lane < row, scaled, jnp.where(lane == row, root, 0.0))
    return upper, inverse


def exact(a, b):
    return jnp.dot(a, b, precision=highest, preferred_element_type=jnp.float32)


def basis_kernel(scale, pair_ref, rows_ref, basis_ref, factor_ref, tile_ref, pivot_ref):
    parts, double, size = pair_ref.shape
    count = double // 2
    high = jnp.concatenate([pair_ref[k, :count, :] for k in range(parts)], axis=0)
    low = jnp.concatenate([pair_ref[k, count:, :] for k in range(parts)], axis=0)
    lane = lax.broadcasted_iota(jnp.int32, (size, size), 1)
    sub = lax.broadcasted_iota(jnp.int32, (size, size), 0)
    diagonal = jnp.where(lane == sub, high, 0.0)
    down = jnp.floor(jnp.log(jnp.max(diagonal, axis=1, keepdims=True)) * (0.5 / math.log(2.0)))
    across = jnp.floor(jnp.log(jnp.max(diagonal, axis=0, keepdims=True)) * (0.5 / math.log(2.0)))
    shrink = power_of_two(-down)
    shrink_across = power_of_two(-across)
    four = jnp.where(shrink > 0.0, 4.0, 8.0)
    high = high * shrink * shrink_across
    low = low * shrink * shrink_across

    upper_first, inverse_first = triangles(high, tile_ref, pivot_ref)

    gram_slices = sliced(high, four, GRAM_SLICES, late=low, late_at=3)
    bound = bound_of(jnp.max(jnp.abs(inverse_first), axis=1, keepdims=True))
    inverse_slices = sliced(inverse_first, bound, INVERSE_SLICES)
    gram_stack = jnp.concatenate(gram_slices, axis=0).astype(jnp.bfloat16)
    inverse_stack = jnp.concatenate(inverse_slices, axis=0).astype(jnp.bfloat16)
    products = lax.dot_general(
        gram_stack, inverse_stack, (((1,), (1,)), ((), ())), preferred_element_type=jnp.float32
    )
    lower_high, lower_low = add_levels(
        block_reader(products, size), GRAM_SLICES, INVERSE_SLICES, 6
    )
    lower_slices = sliced(lower_high, four, FIRST_SLICES, late=lower_low, late_at=3)
    lower_stack = jnp.concatenate(lower_slices, axis=1).astype(jnp.bfloat16)
    products = jnp.dot(inverse_stack, lower_stack, preferred_element_type=jnp.float32)
    gram_second, rest = add_levels(
        block_reader(products, size), INVERSE_SLICES, FIRST_SLICES, 5
    )
    gram_second = gram_second + rest

    upper_second, inverse_second = triangles(gram_second, tile_ref, pivot_ref)
    basis_first = exact(inverse_first, rows_ref[...] * shrink)
    basis = exact(inverse_second, basis_first)
    basis_ref[...] = basis * scale
    factor = exact(upper_second, upper_first)
    factor_ref[...] = factor * (power_of_two(across) * (1.0 / scale))


def in_vmem(kernel, name, out_shape, *operands, scratch=()):
    vmem = pl.BlockSpec(memory_space=pltpu.VMEM)
    single = not isinstance(out_shape, tuple)
    return pl.pallas_call(
        kernel,
        out_shape=out_shape,
        in_specs=[vmem] * len(operands),
        out_specs=vmem if single else tuple(vmem for _ in out_shape),
        scratch_shapes=scratch,
        name=name,
    )(*operands)


def orthonormal(rows, scale):
    size = rows.shape[0]
    parts = lax.axis_size("probe")
    count = 2 * size // parts
    places = lax.axis_size("space")
    pair = jax.ShapeDtypeStruct((parts, count, size), jnp.float32)
    one = jax.ShapeDtypeStruct((count, size), jnp.float32)
    levels = places // CORES
    copies = jax.ShapeDtypeStruct((levels, count, size), jnp.float32)
    gram = in_vmem(gram_kernel, "gram", pair, rows)
    gram = lax.all_to_all(gram, "probe", 0, 0, tiled=True)
    own = in_vmem(sum_kernel, "probe_sum", one, gram)
    other = lax.ppermute(own, "space", [(k, k ^ 1) for k in range(places)])
    spread = in_vmem(spread_kernel, "core_sum", copies, own, other)
    groups = [[core + CORES * k for k in range(levels)] for core in range(CORES)]
    spread = lax.all_to_all(spread, "space", 0, 0, tiled=True, axis_index_groups=groups)
    whole = in_vmem(sum_spread_kernel, "space_sum", pair, spread)
    whole = lax.all_to_all(whole, "probe", 0, 0, tiled=True)
    return in_vmem(
        functools.partial(basis_kernel, scale), "basis",
        (
            jax.ShapeDtypeStruct(rows.shape, jnp.float32),
            jax.ShapeDtypeStruct((size, size), jnp.float32),
        ),
        whole, rows,
        scratch=(pltpu.VMEM((size, size), jnp.float32),) * 2,
    )


def on_device(probes, sensitivity, obs_weight, prior_weight, connectivity):
    node_count = probes.shape[1]
    low = shifted(probes[:, node_count - HALO :], "space", 1)
    high = shifted(probes[:, :HALO], "space", -1)
    images, lower, upper = element_images(
        low, probes, high, connectivity, sensitivity, obs_weight, prior_weight
    )
    lower_rim = shifted(lower, "space", -1)
    upper_rim = shifted(upper, "space", 1)
    images = images.at[:, node_count - HALO :].add(lower_rim)
    images = images.at[:, :HALO].add(upper_rim)
    scale = math.sqrt(float(node_count * lax.axis_size("space")))
    rows = lax.all_to_all(images, "probe", 1, 0, tiled=True)
    basis, factor = orthonormal(rows, scale)
    return lax.all_to_all(basis, "probe", 0, 1, tiled=True), factor


def solution(mesh):
    return jax.shard_map(
        on_device,
        mesh=mesh,
        in_specs=(
            P("probe", "space"),
            P(None, None, "space"),
            P(None, "space"),
            P("space"),
            P(None, "space"),
        ),
        out_specs=(P("probe", "space"), P()),
        check_vma=False,
    )
```

```python
import functools
import math

import jax
import jax.numpy as jnp
from jax import lax
from jax.experimental import pallas as pl
from jax.experimental.pallas import tpu as pltpu
from jax.sharding import PartitionSpec as P

HALO = 128
LANES = 128
WIDE = 256
CORES = 2
TOGETHER = 8

highest = lax.Precision.HIGHEST


def shifted(block, axis, distance):
    devices = range(lax.axis_size(axis))
    route = [(i - distance, i) for i in devices if i - distance in devices]
    return lax.ppermute(block, axis, route)


def selected(candidates, place, bit):
    if len(candidates) == 1:
        return candidates[0]()
    span = 1 << bit
    if len(candidates) <= span:
        return selected(candidates, place, bit - 1)
    low = selected(candidates[:span], place, bit - 1)
    high = selected(candidates[span:], place, bit - 1)
    return jnp.where((place & span) != 0, high, low)


def element_kernel(
    low_ref, probes_ref, high_ref, connectivity_ref, sensitivity_ref, weight_ref, prior_ref,
    images_ref, lower_ref, upper_ref, total_ref,
):
    probe_count, node_count = probes_ref.shape
    corner_count, element_count = connectivity_ref.shape
    gauss_count = sensitivity_ref.shape[0]
    tiles = node_count // LANES + 2
    blocks = tiles * LANES // WIDE
    packed = 2 * probe_count
    thirds = -(-blocks // 2)

    def tile(k):
        if k == 0:
            return low_ref[...]
        if k == tiles - 1:
            return high_ref[...]
        return probes_ref[:, (k - 1) * LANES : k * LANES]

    total_ref[...] = jnp.zeros_like(total_ref)
    row = lax.broadcasted_iota(jnp.int32, (WIDE, LANES), 0).astype(jnp.float32).astype(jnp.bfloat16)
    lower_half = lax.broadcasted_iota(jnp.int32, (packed, LANES), 0) >= probe_count
    lower_half = jnp.where(lower_half, 1.0, 0.0)
    one = jnp.ones((WIDE, LANES), jnp.bfloat16)
    none = jnp.zeros((WIDE, LANES), jnp.bfloat16)
    zero = jnp.zeros((packed, LANES), jnp.bfloat16)
    top_bit = (tiles - 1).bit_length() - 1

    def columns_of(step):
        return pl.ds(pl.multiple_of(step * LANES, LANES), LANES)

    def node_of(corner, step):
        return jnp.broadcast_to(
            connectivity_ref[corner : corner + 1, columns_of(step)], (probe_count, LANES)
        )

    def gather(corner, step):
        node = node_of(corner, step)
        lane = node & (LANES - 1)
        picks = [
            functools.partial(
                lambda k, at: jnp.take_along_axis(tile(k), at, axis=1, mode="promise_in_bounds"),
                k, lane,
            )
            for k in range(tiles)
        ]
        return selected(picks, lax.shift_right_logical(node, 7), top_bit)

    def pull(gathered, step):
        columns = columns_of(step)
        observed = []
        for gauss in range(gauss_count):
            value = gathered[0] * sensitivity_ref[gauss, 0:1, columns]
            for corner in range(1, corner_count):
                value = value + gathered[corner] * sensitivity_ref[gauss, corner : corner + 1, columns]
            observed.append(value * weight_ref[gauss : gauss + 1, columns])
        pulled = []
        for corner in range(corner_count):
            value = observed[0] * sensitivity_ref[0, corner : corner + 1, columns]
            for gauss in range(1, gauss_count):
                value = value + observed[gauss] * sensitivity_ref[gauss, corner : corner + 1, columns]
            pulled.append(value)
        return tuple(pulled)

    def operands(value, corner, step):
        first = value.astype(jnp.bfloat16).astype(jnp.float32)
        rest = value - first
        second = rest.astype(jnp.bfloat16).astype(jnp.float32)
        third = rest - second
        heads = jnp.concatenate([first, second], axis=0).astype(jnp.bfloat16)
        tails = jnp.concatenate([third, third], axis=0).astype(jnp.bfloat16)
        node = node_of(corner, step)
        place = lax.shift_right_logical(node, 8).astype(jnp.float32)
        place = jnp.concatenate([place, place], axis=0)
        offset = (place - lower_half).astype(jnp.bfloat16)
        place = place.astype(jnp.bfloat16)
        parts = []
        for k in range(blocks):
            here = place == jnp.full((packed, LANES), k, jnp.bfloat16)
            parts.append(jnp.where(here, heads, zero))
        for k in range(thirds):
            here = offset == jnp.full((packed, LANES), 2 * k, jnp.bfloat16)
            parts.append(jnp.where(here, tails, zero))
        lane = (node & (WIDE - 1)).astype(jnp.float32)
        lane = jnp.concatenate([lane, lane], axis=0).astype(jnp.bfloat16)
        lane = jnp.concatenate([lane] * (WIDE // packed), axis=0)
        return jnp.concatenate(parts, axis=0), jnp.where(row == lane, one, none)

    last = element_count // LANES - 1

    def trip(step, pulled):
        ahead = jnp.minimum(step + 1, last)
        gathered = []
        for group in range(0, corner_count, TOGETHER):
            left, right = [], []
            for corner in range(group, group + TOGETHER):
                gathered.append(gather(corner, ahead))
                a, b = operands(pulled[corner], corner, step)
                left.append(a)
                right.append(b)
            total_ref[...] += lax.dot_general(
                jnp.concatenate(left, axis=1), jnp.concatenate(right, axis=1),
                (((1,), (1,)), ((), ())), preferred_element_type=jnp.float32,
            )
        return pull(gathered, ahead)

    pulled = pull([gather(corner, 0) for corner in range(corner_count)], 0)
    lax.fori_loop(0, last + 1, trip, pulled)

    for block in range(blocks):
        at = block * packed
        tail = blocks * packed + block * probe_count
        value = total_ref[tail : tail + probe_count, :]
        value = value + total_ref[at + probe_count : at + packed, :]
        value = value + total_ref[at : at + probe_count, :]
        for half in range(WIDE // LANES):
            k = block * (WIDE // LANES) + half
            part = value[:, half * LANES : (half + 1) * LANES]
            if k == 0:
                lower_ref[...] = part
            elif k == tiles - 1:
                upper_ref[...] = part
            else:
                span = slice((k - 1) * LANES, k * LANES)
                images_ref[:, span] = part + prior_ref[:, span] * probes_ref[:, span]


def element_images(low, probes, high, connectivity, sensitivity, obs_weight, prior_weight):
    probe_count, node_count = probes.shape
    corner_count = connectivity.shape[0]
    blocks = (node_count + 2 * HALO) // WIDE
    rows = (blocks + -(-blocks // 2)) * 2 * probe_count
    vmem = pl.BlockSpec(memory_space=pltpu.VMEM)
    rim = jax.ShapeDtypeStruct((probe_count, HALO), jnp.float32)
    return pl.pallas_call(
        element_kernel,
        out_shape=(jax.ShapeDtypeStruct(probes.shape, jnp.float32), rim, rim),
        in_specs=[vmem] * 7,
        out_specs=(vmem, vmem, vmem),
        scratch_shapes=[pltpu.VMEM((rows, WIDE), jnp.float32)],
        name="element_images",
    )(low, probes, high, connectivity, sensitivity, obs_weight, prior_weight.reshape(1, -1))


def rim_kernel(images_ref, lower_ref, upper_ref, sum_ref):
    node_count = images_ref.shape[1]
    sum_ref[...] = images_ref[...]
    sum_ref[:, :HALO] = images_ref[:, :HALO] + upper_ref[...]
    sum_ref[:, node_count - HALO :] = images_ref[:, node_count - HALO :] + lower_ref[...]


SUBLANES = 8
GROUP = 2
SLICE = 2.0**-8
PROBE_SLICES = 4
GRAM_SLICES = 5
INVERSE_SLICES = 4
FIRST_SLICES = 5


def power_of_two(value):
    return jnp.exp(value * math.log(2.0)).astype(jnp.bfloat16).astype(jnp.float32)


def bound_of(magnitude):
    return power_of_two(jnp.floor(jnp.log(magnitude) * (1.0 / math.log(2.0))) + 1.0)


def sliced(value, bound, count, late=None, late_at=0):
    sigma = bound * (1.5 * 2.0**16)
    slices = []
    for k in range(count):
        if late is not None and k == late_at:
            value = value + late
        piece = (value + sigma) - sigma
        slices.append(piece)
        value = value - piece
        sigma = sigma * SLICE
    return slices


def two_sum(a, b):
    total = a + b
    part = total - a
    return total, (a - (total - part)) + (b - part)


def added(left, right):
    total, error = two_sum(left[0], right[0])
    error = error + (left[1] + right[1])
    high = total + error
    return high, error - (high - total)


def add_levels(blocks, rows, columns, levels):
    high = low = None
    for level in range(levels):
        part = None
        for a in range(rows):
            b = level - a
            if 0 <= b < columns:
                part = blocks(a, b) if part is None else part + blocks(a, b)
        if high is None:
            high, low = part, jnp.zeros_like(part)
        else:
            high, error = two_sum(high, part)
            low = low + error
    total = high + low
    return total, low - (total - high)


def block_reader(products, size):
    return lambda a, b: products[a * size : (a + 1) * size, b * size : (b + 1) * size]


def gram_kernel(rows_ref, pair_ref):
    rows = rows_ref[...]
    size = rows.shape[0]
    bound = bound_of(jnp.max(jnp.abs(rows), axis=1, keepdims=True))
    stacked = jnp.concatenate(sliced(rows, bound, PROBE_SLICES), axis=0).astype(jnp.bfloat16)
    products = lax.dot_general(
        stacked, stacked, (((1,), (1,)), ((), ())), preferred_element_type=jnp.float32
    )
    high, low = add_levels(block_reader(products, size), PROBE_SLICES, PROBE_SLICES, 5)
    parts, double, _ = pair_ref.shape
    count = double // 2
    for part in range(parts):
        pair_ref[part, :count, :] = high[part * count : (part + 1) * count, :]
        pair_ref[part, count:, :] = low[part * count : (part + 1) * count, :]


def pairs_added(pairs):
    while len(pairs) > 1:
        joined = [added(a, b) for a, b in zip(pairs[::2], pairs[1::2])]
        pairs = joined + pairs[len(pairs) // 2 * 2 :]
    return pairs[0]


def halves(block):
    count = block.shape[0] // 2
    return block[:count, :], block[count:, :]


def sum_kernel(parts_ref, total_ref):
    high, low = pairs_added([halves(parts_ref[k]) for k in range(parts_ref.shape[0])])
    total_ref[...] = jnp.concatenate([high, low], axis=0)


def spread_kernel(own_ref, other_ref, copies_ref):
    high, low = added(halves(own_ref[...]), halves(other_ref[...]))
    total = jnp.concatenate([high, low], axis=0)
    for k in range(copies_ref.shape[0]):
        copies_ref[k] = total


def sum_spread_kernel(parts_ref, copies_ref):
    high, low = pairs_added([halves(parts_ref[k]) for k in range(parts_ref.shape[0])])
    total = jnp.concatenate([high, low], axis=0)
    for k in range(copies_ref.shape[0]):
        copies_ref[k] = total


def eliminate_group(tiles, pivots, at):
    shape = tiles[0].shape
    lane = lax.broadcasted_iota(jnp.int32, shape, 1)
    sub = lax.broadcasted_iota(jnp.int32, shape, 0)
    chosen = range(GROUP)
    columns = [[jnp.broadcast_to(tile[:, at + r : at + r + 1], shape) for r in chosen] for tile in tiles]
    entry = [
        [jnp.broadcast_to(columns[0][c][at + r : at + r + 1, :], shape) for c in chosen] for r in chosen
    ]
    rows = [jnp.broadcast_to(tiles[0][at + r : at + r + 1, :], shape) for r in chosen]
    factor = [[None] * GROUP for _ in chosen]
    scaled = []
    for s in chosen:
        over = 1.0 / entry[s][s]
        here = lane == at + s
        with_one = jnp.where(here, 1.0, rows[s])
        for r in range(s + 1, GROUP):
            factor[s][r] = entry[s][r] * over
            for c in range(r, GROUP):
                entry[r][c] = entry[r][c] - factor[s][r] * entry[s][c]
            rows[r] = jnp.where(here, 0.0, rows[r]) - factor[s][r] * with_one
        later = (lane > at + s) & (lane < at + GROUP)
        scaled.append(jnp.where(later, 0.0, with_one) * over)
    inside = (lane >= at) & (lane < at + GROUP)
    done = []
    for k, tile in enumerate(tiles):
        clear = inside
        if k == 0:
            below = sub >= at + GROUP
            clear = inside & below
        new = jnp.where(clear, 0.0, tile)
        own = list(columns[k])
        for s in chosen:
            for r in range(s + 1, GROUP):
                own[r] = own[r] - own[s] * factor[s][r]
        for s in chosen:
            value = jnp.where(below, own[s], 0.0) if k == 0 else own[s]
            new = new - value * scaled[s]
        if k == 0:
            for s in chosen:
                new = jnp.where(sub == at + s, rows[s], new)
                pivots = jnp.where(sub == at + s, entry[s][s], pivots)
        done.append(new)
    return done, pivots


def triangles(gram, tile_ref, pivot_ref):
    size = gram.shape[0]
    count = size // SUBLANES
    tiles = [gram[k * SUBLANES : (k + 1) * SUBLANES, :] for k in range(count)]

    def block(step, tiles):
        tiles = list(tiles)
        pivots = jnp.ones((SUBLANES, size), jnp.float32)
        for at in range(0, SUBLANES, GROUP):
            tiles, pivots = eliminate_group(tiles, pivots, at)
        place = pl.ds(pl.multiple_of(step * SUBLANES, SUBLANES), SUBLANES)
        tile_ref[place, :] = pltpu.roll(tiles[0], step * SUBLANES, 1)
        pivot_ref[place, :] = pivots
        tiles = [pltpu.roll(tile, size - SUBLANES, 1) for tile in tiles]
        return tuple(tiles[1:] + tiles[:1])

    half = count // 2
    tiles = lax.fori_loop(0, half, block, tuple(tiles))
    lax.fori_loop(half, count, block, tuple(tiles[:half]))
    tile, pivot = tile_ref[...], pivot_ref[...]
    lane = lax.broadcasted_iota(jnp.int32, tile.shape, 1)
    row = lax.broadcasted_iota(jnp.int32, tile.shape, 0)
    root = lax.rsqrt(pivot)
    root = root * (1.5 - 0.5 * pivot * root * root)
    scaled = tile * root
    upper = jnp.where(lane > row, scaled, jnp.where(lane == row, pivot * root, 0.0))
    inverse = jnp.where(lane < row, scaled, jnp.where(lane == row, root, 0.0))
    return upper, inverse


def exact(a, b):
    return jnp.dot(a, b, precision=highest, preferred_element_type=jnp.float32)


def basis_kernel(scale, pair_ref, rows_ref, basis_ref, factor_ref, tile_ref, pivot_ref):
    parts, double, size = pair_ref.shape
    count = double // 2
    high = jnp.concatenate([pair_ref[k, :count, :] for k in range(parts)], axis=0)
    low = jnp.concatenate([pair_ref[k, count:, :] for k in range(parts)], axis=0)
    lane = lax.broadcasted_iota(jnp.int32, (size, size), 1)
    sub = lax.broadcasted_iota(jnp.int32, (size, size), 0)
    diagonal = jnp.where(lane == sub, high, 0.0)
    down = jnp.floor(jnp.log(jnp.max(diagonal, axis=1, keepdims=True)) * (0.5 / math.log(2.0)))
    across = jnp.floor(jnp.log(jnp.max(diagonal, axis=0, keepdims=True)) * (0.5 / math.log(2.0)))
    shrink = power_of_two(-down)
    shrink_across = power_of_two(-across)
    four = jnp.where(shrink > 0.0, 4.0, 8.0)
    high = high * shrink * shrink_across
    low = low * shrink * shrink_across

    upper_first, inverse_first = triangles(high, tile_ref, pivot_ref)

    gram_slices = sliced(high, four, GRAM_SLICES, late=low, late_at=3)
    bound = bound_of(jnp.max(jnp.abs(inverse_first), axis=1, keepdims=True))
    inverse_slices = sliced(inverse_first, bound, INVERSE_SLICES)
    gram_stack = jnp.concatenate(gram_slices, axis=0).astype(jnp.bfloat16)
    inverse_stack = jnp.concatenate(inverse_slices, axis=0).astype(jnp.bfloat16)
    products = lax.dot_general(
        gram_stack, inverse_stack, (((1,), (1,)), ((), ())), preferred_element_type=jnp.float32
    )
    lower_high, lower_low = add_levels(
        block_reader(products, size), GRAM_SLICES, INVERSE_SLICES, 6
    )
    lower_slices = sliced(lower_high, four, FIRST_SLICES, late=lower_low, late_at=3)
    lower_stack = jnp.concatenate(lower_slices, axis=1).astype(jnp.bfloat16)
    products = jnp.dot(inverse_stack, lower_stack, preferred_element_type=jnp.float32)
    gram_second, rest = add_levels(
        block_reader(products, size), INVERSE_SLICES, FIRST_SLICES, 5
    )
    gram_second = gram_second + rest

    upper_second, inverse_second = triangles(gram_second, tile_ref, pivot_ref)
    basis_first = exact(inverse_first, rows_ref[...] * shrink)
    basis = exact(inverse_second, basis_first)
    basis_ref[...] = basis * scale
    factor = exact(upper_second, upper_first)
    factor_ref[...] = factor * (power_of_two(across) * (1.0 / scale))


def in_vmem(kernel, name, out_shape, *operands, scratch=()):
    vmem = pl.BlockSpec(memory_space=pltpu.VMEM)
    single = not isinstance(out_shape, tuple)
    return pl.pallas_call(
        kernel,
        out_shape=out_shape,
        in_specs=[vmem] * len(operands),
        out_specs=vmem if single else tuple(vmem for _ in out_shape),
        scratch_shapes=scratch,
        name=name,
    )(*operands)


def orthonormal(rows, scale):
    size = rows.shape[0]
    parts = lax.axis_size("probe")
    count = 2 * size // parts
    places = lax.axis_size("space")
    pair = jax.ShapeDtypeStruct((parts, count, size), jnp.float32)
    one = jax.ShapeDtypeStruct((count, size), jnp.float32)
    levels = places // CORES
    copies = jax.ShapeDtypeStruct((levels, count, size), jnp.float32)
    gram = in_vmem(gram_kernel, "gram", pair, rows)
    gram = lax.all_to_all(gram, "probe", 0, 0, tiled=True)
    own = in_vmem(sum_kernel, "probe_sum", one, gram)
    other = lax.ppermute(own, "space", [(k, k ^ 1) for k in range(places)])
    spread = in_vmem(spread_kernel, "core_sum", copies, own, other)
    groups = [[core + CORES * k for k in range(levels)] for core in range(CORES)]
    spread = lax.all_to_all(spread, "space", 0, 0, tiled=True, axis_index_groups=groups)
    whole = in_vmem(sum_spread_kernel, "space_sum", pair, spread)
    whole = lax.all_to_all(whole, "probe", 0, 0, tiled=True)
    return in_vmem(
        functools.partial(basis_kernel, scale), "basis",
        (
            jax.ShapeDtypeStruct(rows.shape, jnp.float32),
            jax.ShapeDtypeStruct((size, size), jnp.float32),
        ),
        whole, rows,
        scratch=(pltpu.VMEM((size, size), jnp.float32),) * 2,
    )


def on_device(probes, sensitivity, obs_weight, prior_weight, connectivity):
    node_count = probes.shape[1]
    low = shifted(probes[:, node_count - HALO :], "space", 1)
    high = shifted(probes[:, :HALO], "space", -1)
    images, lower, upper = element_images(
        low, probes, high, connectivity, sensitivity, obs_weight, prior_weight
    )
    lower_rim = shifted(lower, "space", -1)
    upper_rim = shifted(upper, "space", 1)
    images = in_vmem(
        rim_kernel, "rims", jax.ShapeDtypeStruct(images.shape, jnp.float32),
        images, lower_rim, upper_rim,
    )
    scale = math.sqrt(float(node_count * lax.axis_size("space")))
    rows = lax.all_to_all(images, "probe", 1, 0, tiled=True)
    basis, factor = orthonormal(rows, scale)
    return lax.all_to_all(basis, "probe", 0, 1, tiled=True), factor


def solution(mesh):
    return jax.shard_map(
        on_device,
        mesh=mesh,
        in_specs=(
            P("probe", "space"),
            P(None, None, "space"),
            P(None, "space"),
            P("space"),
            P(None, "space"),
        ),
        out_specs=(P("probe", "space"), P()),
        check_vma=False,
    )
```

```python
import functools
import math

import jax
import jax.numpy as jnp
from jax import lax
from jax.experimental import pallas as pl
from jax.experimental.pallas import tpu as pltpu
from jax.sharding import PartitionSpec as P

HALO = 128
LANES = 128
WIDE = 256
CORES = 2
TOGETHER = 8

highest = lax.Precision.HIGHEST


def shifted(block, axis, distance):
    devices = range(lax.axis_size(axis))
    route = [(i - distance, i) for i in devices if i - distance in devices]
    return lax.ppermute(block, axis, route)


def selected(candidates, place, bit):
    if len(candidates) == 1:
        return candidates[0]()
    span = 1 << bit
    if len(candidates) <= span:
        return selected(candidates, place, bit - 1)
    low = selected(candidates[:span], place, bit - 1)
    high = selected(candidates[span:], place, bit - 1)
    return jnp.where((place & span) != 0, high, low)


def element_kernel(
    low_ref, probes_ref, high_ref, connectivity_ref, sensitivity_ref, weight_ref, prior_ref,
    images_ref, lower_ref, upper_ref, total_ref,
):
    probe_count, node_count = probes_ref.shape
    corner_count, element_count = connectivity_ref.shape
    gauss_count = sensitivity_ref.shape[0]
    tiles = node_count // LANES + 2
    blocks = tiles * LANES // WIDE
    packed = 2 * probe_count
    thirds = -(-blocks // 2)

    def tile(k):
        if k == 0:
            return low_ref[...]
        if k == tiles - 1:
            return high_ref[...]
        return probes_ref[:, (k - 1) * LANES : k * LANES]

    total_ref[...] = jnp.zeros_like(total_ref)
    row = lax.broadcasted_iota(jnp.int32, (WIDE, LANES), 0).astype(jnp.float32).astype(jnp.bfloat16)
    lower_half = lax.broadcasted_iota(jnp.int32, (packed, LANES), 0) >= probe_count
    lower_half = jnp.where(lower_half, 1.0, 0.0)
    one = jnp.ones((WIDE, LANES), jnp.bfloat16)
    none = jnp.zeros((WIDE, LANES), jnp.bfloat16)
    zero = jnp.zeros((packed, LANES), jnp.bfloat16)
    top_bit = (tiles - 1).bit_length() - 1

    def columns_of(step):
        return pl.ds(pl.multiple_of(step * LANES, LANES), LANES)

    def node_of(corner, step):
        return jnp.broadcast_to(
            connectivity_ref[corner : corner + 1, columns_of(step)], (probe_count, LANES)
        )

    def gather(corner, step):
        node = node_of(corner, step)
        lane = node & (LANES - 1)
        picks = [
            functools.partial(
                lambda k, at: jnp.take_along_axis(tile(k), at, axis=1, mode="promise_in_bounds"),
                k, lane,
            )
            for k in range(tiles)
        ]
        return selected(picks, lax.shift_right_logical(node, 7), top_bit)

    def pull(gathered, step):
        columns = columns_of(step)
        observed = []
        for gauss in range(gauss_count):
            value = gathered[0] * sensitivity_ref[gauss, 0:1, columns]
            for corner in range(1, corner_count):
                value = value + gathered[corner] * sensitivity_ref[gauss, corner : corner + 1, columns]
            observed.append(value * weight_ref[gauss : gauss + 1, columns])
        pulled = []
        for corner in range(corner_count):
            value = observed[0] * sensitivity_ref[0, corner : corner + 1, columns]
            for gauss in range(1, gauss_count):
                value = value + observed[gauss] * sensitivity_ref[gauss, corner : corner + 1, columns]
            pulled.append(value)
        return tuple(pulled)

    def operands(value, corner, step):
        first = value.astype(jnp.bfloat16).astype(jnp.float32)
        rest = value - first
        second = rest.astype(jnp.bfloat16).astype(jnp.float32)
        third = rest - second
        heads = jnp.concatenate([first, second], axis=0).astype(jnp.bfloat16)
        tails = jnp.concatenate([third, third], axis=0).astype(jnp.bfloat16)
        node = node_of(corner, step)
        place = lax.shift_right_logical(node, 8).astype(jnp.float32)
        place = jnp.concatenate([place, place], axis=0)
        offset = (place - lower_half).astype(jnp.bfloat16)
        place = place.astype(jnp.bfloat16)
        parts = []
        for k in range(blocks):
            here = place == jnp.full((packed, LANES), k, jnp.bfloat16)
            parts.append(jnp.where(here, heads, zero))
        for k in range(thirds):
            here = offset == jnp.full((packed, LANES), 2 * k, jnp.bfloat16)
            parts.append(jnp.where(here, tails, zero))
        lane = (node & (WIDE - 1)).astype(jnp.float32)
        lane = jnp.concatenate([lane, lane], axis=0).astype(jnp.bfloat16)
        lane = jnp.concatenate([lane] * (WIDE // packed), axis=0)
        return jnp.concatenate(parts, axis=0), jnp.where(row == lane, one, none)

    last = element_count // LANES - 1

    def trip(step, pulled):
        ahead = jnp.minimum(step + 1, last)
        gathered = []
        for group in range(0, corner_count, TOGETHER):
            left, right = [], []
            for corner in range(group, group + TOGETHER):
                gathered.append(gather(corner, ahead))
                a, b = operands(pulled[corner], corner, step)
                left.append(a)
                right.append(b)
            total_ref[...] += lax.dot_general(
                jnp.concatenate(left, axis=1), jnp.concatenate(right, axis=1),
                (((1,), (1,)), ((), ())), preferred_element_type=jnp.float32,
            )
        return pull(gathered, ahead)

    pulled = pull([gather(corner, 0) for corner in range(corner_count)], 0)
    lax.fori_loop(0, last + 1, trip, pulled)

    for block in range(blocks):
        at = block * packed
        tail = blocks * packed + block * probe_count
        value = total_ref[tail : tail + probe_count, :]
        value = value + total_ref[at + probe_count : at + packed, :]
        value = value + total_ref[at : at + probe_count, :]
        for half in range(WIDE // LANES):
            k = block * (WIDE // LANES) + half
            part = value[:, half * LANES : (half + 1) * LANES]
            if k == 0:
                lower_ref[...] = part
            elif k == tiles - 1:
                upper_ref[...] = part
            else:
                span = slice((k - 1) * LANES, k * LANES)
                images_ref[:, span] = part + prior_ref[:, span] * probes_ref[:, span]


def element_images(low, probes, high, connectivity, sensitivity, obs_weight, prior_weight):
    probe_count, node_count = probes.shape
    corner_count = connectivity.shape[0]
    blocks = (node_count + 2 * HALO) // WIDE
    rows = (blocks + -(-blocks // 2)) * 2 * probe_count
    vmem = pl.BlockSpec(memory_space=pltpu.VMEM)
    rim = jax.ShapeDtypeStruct((probe_count, HALO), jnp.float32)
    return pl.pallas_call(
        element_kernel,
        out_shape=(jax.ShapeDtypeStruct(probes.shape, jnp.float32), rim, rim),
        in_specs=[vmem] * 7,
        out_specs=(vmem, vmem, vmem),
        scratch_shapes=[pltpu.VMEM((rows, WIDE), jnp.float32)],
        name="element_images",
    )(low, probes, high, connectivity, sensitivity, obs_weight, prior_weight.reshape(1, -1))


SUBLANES = 8
GROUP = 2
PART = 32
SLICE = 2.0**-8
PROBE_SLICES = 4
GRAM_SLICES = 5
INVERSE_SLICES = 4
FIRST_SLICES = 5


def power_of_two(value):
    return jnp.exp(value * math.log(2.0)).astype(jnp.bfloat16).astype(jnp.float32)


def bound_of(magnitude):
    return power_of_two(jnp.floor(jnp.log(magnitude) * (1.0 / math.log(2.0))) + 1.0)


def sliced(value, bound, count, late=None, late_at=0):
    sigma = bound * (1.5 * 2.0**16)
    slices = []
    for k in range(count):
        if late is not None and k == late_at:
            value = value + late
        piece = (value + sigma) - sigma
        slices.append(piece)
        value = value - piece
        sigma = sigma * SLICE
    return slices


def two_sum(a, b):
    total = a + b
    part = total - a
    return total, (a - (total - part)) + (b - part)


def added(left, right):
    total, error = two_sum(left[0], right[0])
    error = error + (left[1] + right[1])
    high = total + error
    return high, error - (high - total)


def add_levels(blocks, rows, columns, levels):
    high = low = None
    for level in range(levels):
        part = None
        for a in range(rows):
            b = level - a
            if 0 <= b < columns:
                part = blocks(a, b) if part is None else part + blocks(a, b)
        if high is None:
            high, low = part, jnp.zeros_like(part)
        else:
            high, error = two_sum(high, part)
            low = low + error
    total = high + low
    return total, low - (total - high)


def block_reader(products, size):
    return lambda a, b: products[a * size : (a + 1) * size, b * size : (b + 1) * size]


def gram_kernel(rows_ref, pair_ref):
    rows = rows_ref[...]
    size = rows.shape[0]
    bound = bound_of(jnp.max(jnp.abs(rows), axis=1, keepdims=True))
    stacked = jnp.concatenate(sliced(rows, bound, PROBE_SLICES), axis=0).astype(jnp.bfloat16)
    products = lax.dot_general(
        stacked, stacked, (((1,), (1,)), ((), ())), preferred_element_type=jnp.float32
    )
    high, low = add_levels(block_reader(products, size), PROBE_SLICES, PROBE_SLICES, 5)
    parts, double, _ = pair_ref.shape
    count = double // 2
    for part in range(parts):
        pair_ref[part, :count, :] = high[part * count : (part + 1) * count, :]
        pair_ref[part, count:, :] = low[part * count : (part + 1) * count, :]


def pairs_added(pairs):
    while len(pairs) > 1:
        joined = [added(a, b) for a, b in zip(pairs[::2], pairs[1::2])]
        pairs = joined + pairs[len(pairs) // 2 * 2 :]
    return pairs[0]


def halves(block):
    count = block.shape[0] // 2
    return block[:count, :], block[count:, :]


def sum_kernel(parts_ref, total_ref):
    high, low = pairs_added([halves(parts_ref[k]) for k in range(parts_ref.shape[0])])
    total_ref[...] = jnp.concatenate([high, low], axis=0)


def spread_kernel(own_ref, other_ref, copies_ref):
    high, low = added(halves(own_ref[...]), halves(other_ref[...]))
    total = jnp.concatenate([high, low], axis=0)
    for k in range(copies_ref.shape[0]):
        copies_ref[k] = total


def sum_spread_kernel(parts_ref, copies_ref):
    high, low = pairs_added([halves(parts_ref[k]) for k in range(parts_ref.shape[0])])
    total = jnp.concatenate([high, low], axis=0)
    for k in range(copies_ref.shape[0]):
        copies_ref[k] = total


def eliminate_group(tiles, pivots, at):
    shape = tiles[0].shape
    lane = lax.broadcasted_iota(jnp.int32, shape, 1)
    sub = lax.broadcasted_iota(jnp.int32, shape, 0)
    chosen = range(GROUP)
    columns = [[jnp.broadcast_to(tile[:, at + r : at + r + 1], shape) for r in chosen] for tile in tiles]
    entry = [
        [jnp.broadcast_to(columns[0][c][at + r : at + r + 1, :], shape) for c in chosen] for r in chosen
    ]
    rows = [jnp.broadcast_to(tiles[0][at + r : at + r + 1, :], shape) for r in chosen]
    factor = [[None] * GROUP for _ in chosen]
    scaled = []
    for s in chosen:
        over = 1.0 / entry[s][s]
        here = lane == at + s
        with_one = jnp.where(here, 1.0, rows[s])
        for r in range(s + 1, GROUP):
            factor[s][r] = entry[s][r] * over
            for c in range(r, GROUP):
                entry[r][c] = entry[r][c] - factor[s][r] * entry[s][c]
            rows[r] = jnp.where(here, 0.0, rows[r]) - factor[s][r] * with_one
        later = (lane > at + s) & (lane < at + GROUP)
        scaled.append(jnp.where(later, 0.0, with_one) * over)
    inside = (lane >= at) & (lane < at + GROUP)
    done = []
    for k, tile in enumerate(tiles):
        clear = inside
        if k == 0:
            below = sub >= at + GROUP
            clear = inside & below
        new = jnp.where(clear, 0.0, tile)
        own = list(columns[k])
        for s in chosen:
            for r in range(s + 1, GROUP):
                own[r] = own[r] - own[s] * factor[s][r]
        for s in chosen:
            value = jnp.where(below, own[s], 0.0) if k == 0 else own[s]
            new = new - value * scaled[s]
        if k == 0:
            for s in chosen:
                new = jnp.where(sub == at + s, rows[s], new)
                pivots = jnp.where(sub == at + s, entry[s][s], pivots)
        done.append(new)
    return done, pivots


def eliminate(work_ref, tile_ref, pivot_ref, upper_ref, inverse_ref):
    size = work_ref.shape[0]
    count = size // SUBLANES
    tiles = [work_ref[k * SUBLANES : (k + 1) * SUBLANES, :] for k in range(count)]

    def block(step, tiles):
        tiles = list(tiles)
        pivots = jnp.ones((SUBLANES, size), jnp.float32)
        for at in range(0, SUBLANES, GROUP):
            tiles, pivots = eliminate_group(tiles, pivots, at)
        place = pl.ds(pl.multiple_of(step * SUBLANES, SUBLANES), SUBLANES)
        tile_ref[place, :] = pltpu.roll(tiles[0], step * SUBLANES, 1)
        pivot_ref[place, :] = pivots
        tiles = [pltpu.roll(tile, size - SUBLANES, 1) for tile in tiles]
        return tuple(tiles[1:] + tiles[:1])

    half = count // 2
    tiles = lax.fori_loop(0, half, block, tuple(tiles))
    lax.fori_loop(half, count, block, tuple(tiles[:half]))
    tile, pivot = tile_ref[...], pivot_ref[...]
    lane = lax.broadcasted_iota(jnp.int32, tile.shape, 1)
    row = lax.broadcasted_iota(jnp.int32, tile.shape, 0)
    root = lax.rsqrt(pivot)
    root = root * (1.5 - 0.5 * pivot * root * root)
    scaled = tile * root
    upper_ref[...] = jnp.where(lane > row, scaled, jnp.where(lane == row, pivot * root, 0.0))
    inverse_ref[...] = jnp.where(lane < row, scaled, jnp.where(lane == row, root, 0.0))


def second_gram(work_ref, low_ref, inverse_ref, gram_ref, slice_ref, lower_ref, one_ref, two_ref):
    size = work_ref.shape[0]

    def part(step):
        return pl.ds(pl.multiple_of(step * PART, PART), PART)

    def shifted_part(a, step):
        return pl.ds(pl.multiple_of(a * size + step * PART, PART), PART)

    def four_where(value):
        return jnp.where(jnp.max(jnp.abs(value), axis=1, keepdims=True) > 0.0, 4.0, 8.0)

    def cut(step, carry):
        high, low, inverse = work_ref[part(step), :], low_ref[part(step), :], inverse_ref[part(step), :]
        for a, piece in enumerate(sliced(high, four_where(high), GRAM_SLICES, late=low, late_at=3)):
            gram_ref[shifted_part(a, step), :] = piece.astype(jnp.bfloat16)
        bound = bound_of(jnp.max(jnp.abs(inverse), axis=1, keepdims=True))
        for a, piece in enumerate(sliced(inverse, bound, INVERSE_SLICES)):
            slice_ref[shifted_part(a, step), :] = piece.astype(jnp.bfloat16)
        return carry

    def lower(step, carry):
        high, low = add_levels(
            lambda a, b: one_ref[shifted_part(a, step), b * size : (b + 1) * size],
            GRAM_SLICES, INVERSE_SLICES, 6,
        )
        for b, piece in enumerate(sliced(high, four_where(high), FIRST_SLICES, late=low, late_at=3)):
            lower_ref[part(step), b * size : (b + 1) * size] = piece.astype(jnp.bfloat16)
        return carry

    def total(step, carry):
        high, low = add_levels(
            lambda a, b: two_ref[shifted_part(a, step), b * size : (b + 1) * size],
            INVERSE_SLICES, FIRST_SLICES, 5,
        )
        work_ref[part(step), :] = high + low
        return carry

    parts = size // PART
    lax.fori_loop(0, parts, cut, 0)
    one_ref[...] = lax.dot_general(
        gram_ref[...], slice_ref[...], (((1,), (1,)), ((), ())), preferred_element_type=jnp.float32
    )
    lax.fori_loop(0, parts, lower, 0)
    two_ref[...] = jnp.dot(slice_ref[...], lower_ref[...], preferred_element_type=jnp.float32)
    lax.fori_loop(0, parts, total, 0)


def basis_kernel(
    scale, pair_ref, rows_ref, basis_ref, factor_ref,
    work_ref, low_ref, tile_ref, pivot_ref, factors_ref, values_ref,
    gram_ref, slice_ref, lower_ref, one_ref, two_ref,
):
    parts, double, size = pair_ref.shape
    count = double // 2
    high = jnp.concatenate([pair_ref[k, :count, :] for k in range(parts)], axis=0)
    low = jnp.concatenate([pair_ref[k, count:, :] for k in range(parts)], axis=0)
    lane = lax.broadcasted_iota(jnp.int32, (size, size), 1)
    sub = lax.broadcasted_iota(jnp.int32, (size, size), 0)
    diagonal = jnp.where(lane == sub, high, 0.0)
    down = jnp.floor(jnp.log(jnp.max(diagonal, axis=1, keepdims=True)) * (0.5 / math.log(2.0)))
    across = jnp.floor(jnp.log(jnp.max(diagonal, axis=0, keepdims=True)) * (0.5 / math.log(2.0)))
    shrink = power_of_two(-down)
    shrink_across = power_of_two(-across)
    work_ref[...] = high * shrink * shrink_across
    low_ref[...] = low * shrink * shrink_across
    grow = power_of_two(across) * (1.0 / scale)
    for k in range(2):
        values_ref[k] = rows_ref[:, k * size : (k + 1) * size] * shrink

    def each(step, carry):
        eliminate(work_ref, tile_ref, pivot_ref, factors_ref.at[2 + step], factors_ref.at[step])

        @pl.when(step == 0)
        def _():
            values_ref[4] = factors_ref[2]
            second_gram(
                work_ref, low_ref, factors_ref.at[0], gram_ref, slice_ref, lower_ref, one_ref, two_ref
            )

        return carry

    lax.fori_loop(0, 2, each, 0)

    def multiply(step, carry):
        late = (step >= 2).astype(jnp.int32)
        last = (step >= 4).astype(jnp.int32)
        values_ref[step + 2 + late] = jnp.dot(
            factors_ref[late + 2 * last], values_ref[step],
            precision=highest, preferred_element_type=jnp.float32,
        )
        return carry

    lax.fori_loop(0, 5, multiply, 0)
    for k in range(2):
        basis_ref[:, k * size : (k + 1) * size] = values_ref[5 + k] * scale
    factor_ref[...] = values_ref[7] * grow


def basis_scratch(size):
    square = pltpu.VMEM((size, size), jnp.float32)
    return (
        square, square, square, square,
        pltpu.VMEM((4, size, size), jnp.float32),
        pltpu.VMEM((8, size, size), jnp.float32),
        pltpu.VMEM((GRAM_SLICES * size, size), jnp.bfloat16),
        pltpu.VMEM((INVERSE_SLICES * size, size), jnp.bfloat16),
        pltpu.VMEM((size, FIRST_SLICES * size), jnp.bfloat16),
        pltpu.VMEM((GRAM_SLICES * size, INVERSE_SLICES * size), jnp.float32),
        pltpu.VMEM((INVERSE_SLICES * size, FIRST_SLICES * size), jnp.float32),
    )


def in_vmem(kernel, name, out_shape, *operands, scratch=()):
    vmem = pl.BlockSpec(memory_space=pltpu.VMEM)
    single = not isinstance(out_shape, tuple)
    return pl.pallas_call(
        kernel,
        out_shape=out_shape,
        in_specs=[vmem] * len(operands),
        out_specs=vmem if single else tuple(vmem for _ in out_shape),
        scratch_shapes=scratch,
        name=name,
    )(*operands)


def orthonormal(rows, scale):
    size = rows.shape[0]
    parts = lax.axis_size("probe")
    count = 2 * size // parts
    places = lax.axis_size("space")
    pair = jax.ShapeDtypeStruct((parts, count, size), jnp.float32)
    one = jax.ShapeDtypeStruct((count, size), jnp.float32)
    levels = places // CORES
    copies = jax.ShapeDtypeStruct((levels, count, size), jnp.float32)
    gram = in_vmem(gram_kernel, "gram", pair, rows)
    gram = lax.all_to_all(gram, "probe", 0, 0, tiled=True)
    own = in_vmem(sum_kernel, "probe_sum", one, gram)
    other = lax.ppermute(own, "space", [(k, k ^ 1) for k in range(places)])
    spread = in_vmem(spread_kernel, "core_sum", copies, own, other)
    groups = [[core + CORES * k for k in range(levels)] for core in range(CORES)]
    spread = lax.all_to_all(spread, "space", 0, 0, tiled=True, axis_index_groups=groups)
    whole = in_vmem(sum_spread_kernel, "space_sum", pair, spread)
    whole = lax.all_to_all(whole, "probe", 0, 0, tiled=True)
    return in_vmem(
        functools.partial(basis_kernel, scale), "basis",
        (
            jax.ShapeDtypeStruct(rows.shape, jnp.float32),
            jax.ShapeDtypeStruct((size, size), jnp.float32),
        ),
        whole, rows,
        scratch=basis_scratch(size),
    )


def on_device(probes, sensitivity, obs_weight, prior_weight, connectivity):
    node_count = probes.shape[1]
    low = shifted(probes[:, node_count - HALO :], "space", 1)
    high = shifted(probes[:, :HALO], "space", -1)
    images, lower, upper = element_images(
        low, probes, high, connectivity, sensitivity, obs_weight, prior_weight
    )
    lower_rim = shifted(lower, "space", -1)
    upper_rim = shifted(upper, "space", 1)
    images = jnp.concatenate(
        [
            images[:, :HALO] + upper_rim,
            images[:, HALO : node_count - HALO],
            images[:, node_count - HALO :] + lower_rim,
        ],
        axis=1,
    )
    scale = math.sqrt(float(node_count * lax.axis_size("space")))
    rows = lax.all_to_all(images, "probe", 1, 0, tiled=True)
    basis, factor = orthonormal(rows, scale)
    return lax.all_to_all(basis, "probe", 0, 1, tiled=True), factor


def solution(mesh):
    return jax.shard_map(
        on_device,
        mesh=mesh,
        in_specs=(
            P("probe", "space"),
            P(None, None, "space"),
            P(None, "space"),
            P("space"),
            P(None, "space"),
        ),
        out_specs=(P("probe", "space"), P()),
        check_vma=False,
    )
```

```python
import functools
import math

import jax
import jax.numpy as jnp
from jax import lax
from jax.experimental import pallas as pl
from jax.experimental.pallas import tpu as pltpu
from jax.sharding import PartitionSpec as P

HALO = 128
LANES = 128
WIDE = 256
CORES = 2
TOGETHER = 8

highest = lax.Precision.HIGHEST


def shifted(block, axis, distance):
    devices = range(lax.axis_size(axis))
    route = [(i - distance, i) for i in devices if i - distance in devices]
    return lax.ppermute(block, axis, route)


def selected(candidates, place, bit):
    if len(candidates) == 1:
        return candidates[0]()
    span = 1 << bit
    if len(candidates) <= span:
        return selected(candidates, place, bit - 1)
    low = selected(candidates[:span], place, bit - 1)
    high = selected(candidates[span:], place, bit - 1)
    return jnp.where((place & span) != 0, high, low)


def element_kernel(
    low_ref, probes_ref, high_ref, connectivity_ref, sensitivity_ref, weight_ref, prior_ref,
    images_ref, lower_ref, upper_ref, total_ref,
):
    probe_count, node_count = probes_ref.shape
    corner_count, element_count = connectivity_ref.shape
    gauss_count = sensitivity_ref.shape[0]
    tiles = node_count // LANES + 2
    blocks = tiles * LANES // WIDE
    packed = 2 * probe_count
    thirds = -(-blocks // 2)

    def tile(k):
        if k == 0:
            return low_ref[...]
        if k == tiles - 1:
            return high_ref[...]
        return probes_ref[:, (k - 1) * LANES : k * LANES]

    total_ref[...] = jnp.zeros_like(total_ref)
    row = lax.broadcasted_iota(jnp.int32, (WIDE, LANES), 0).astype(jnp.float32).astype(jnp.bfloat16)
    lower_half = lax.broadcasted_iota(jnp.int32, (packed, LANES), 0) >= probe_count
    lower_half = jnp.where(lower_half, 1.0, 0.0)
    one = jnp.ones((WIDE, LANES), jnp.bfloat16)
    none = jnp.zeros((WIDE, LANES), jnp.bfloat16)
    zero = jnp.zeros((packed, LANES), jnp.bfloat16)
    top_bit = (tiles - 1).bit_length() - 1

    def columns_of(step):
        return pl.ds(pl.multiple_of(step * LANES, LANES), LANES)

    def node_of(corner, step):
        return jnp.broadcast_to(
            connectivity_ref[corner : corner + 1, columns_of(step)], (probe_count, LANES)
        )

    def gather(corner, step):
        node = node_of(corner, step)
        lane = node & (LANES - 1)
        picks = [
            functools.partial(
                lambda k, at: jnp.take_along_axis(tile(k), at, axis=1, mode="promise_in_bounds"),
                k, lane,
            )
            for k in range(tiles)
        ]
        return selected(picks, lax.shift_right_logical(node, 7), top_bit)

    def pull(gathered, step):
        columns = columns_of(step)
        observed = []
        for gauss in range(gauss_count):
            value = gathered[0] * sensitivity_ref[gauss, 0:1, columns]
            for corner in range(1, corner_count):
                value = value + gathered[corner] * sensitivity_ref[gauss, corner : corner + 1, columns]
            observed.append(value * weight_ref[gauss : gauss + 1, columns])
        pulled = []
        for corner in range(corner_count):
            value = observed[0] * sensitivity_ref[0, corner : corner + 1, columns]
            for gauss in range(1, gauss_count):
                value = value + observed[gauss] * sensitivity_ref[gauss, corner : corner + 1, columns]
            pulled.append(value)
        return tuple(pulled)

    def operands(value, corner, step):
        first = value.astype(jnp.bfloat16).astype(jnp.float32)
        rest = value - first
        second = rest.astype(jnp.bfloat16).astype(jnp.float32)
        third = rest - second
        heads = jnp.concatenate([first, second], axis=0).astype(jnp.bfloat16)
        tails = jnp.concatenate([third, third], axis=0).astype(jnp.bfloat16)
        node = node_of(corner, step)
        place = lax.shift_right_logical(node, 8).astype(jnp.float32)
        place = jnp.concatenate([place, place], axis=0)
        offset = (place - lower_half).astype(jnp.bfloat16)
        place = place.astype(jnp.bfloat16)
        parts = []
        for k in range(blocks):
            here = place == jnp.full((packed, LANES), k, jnp.bfloat16)
            parts.append(jnp.where(here, heads, zero))
        for k in range(thirds):
            here = offset == jnp.full((packed, LANES), 2 * k, jnp.bfloat16)
            parts.append(jnp.where(here, tails, zero))
        lane = (node & (WIDE - 1)).astype(jnp.float32)
        lane = jnp.concatenate([lane, lane], axis=0).astype(jnp.bfloat16)
        lane = jnp.concatenate([lane] * (WIDE // packed), axis=0)
        return jnp.concatenate(parts, axis=0), jnp.where(row == lane, one, none)

    last = element_count // LANES - 1

    def trip(step, pulled):
        ahead = jnp.minimum(step + 1, last)
        gathered = []
        for group in range(0, corner_count, TOGETHER):
            left, right = [], []
            for corner in range(group, group + TOGETHER):
                gathered.append(gather(corner, ahead))
                a, b = operands(pulled[corner], corner, step)
                left.append(a)
                right.append(b)
            total_ref[...] += lax.dot_general(
                jnp.concatenate(left, axis=1), jnp.concatenate(right, axis=1),
                (((1,), (1,)), ((), ())), preferred_element_type=jnp.float32,
            )
        return pull(gathered, ahead)

    pulled = pull([gather(corner, 0) for corner in range(corner_count)], 0)
    lax.fori_loop(0, last + 1, trip, pulled)

    for block in range(blocks):
        at = block * packed
        tail = blocks * packed + block * probe_count
        value = total_ref[tail : tail + probe_count, :]
        value = value + total_ref[at + probe_count : at + packed, :]
        value = value + total_ref[at : at + probe_count, :]
        for half in range(WIDE // LANES):
            k = block * (WIDE // LANES) + half
            part = value[:, half * LANES : (half + 1) * LANES]
            if k == 0:
                lower_ref[...] = part
            elif k == tiles - 1:
                upper_ref[...] = part
            else:
                span = slice((k - 1) * LANES, k * LANES)
                images_ref[:, span] = part + prior_ref[:, span] * probes_ref[:, span]


def element_images(low, probes, high, connectivity, sensitivity, obs_weight, prior_weight):
    probe_count, node_count = probes.shape
    corner_count = connectivity.shape[0]
    blocks = (node_count + 2 * HALO) // WIDE
    rows = (blocks + -(-blocks // 2)) * 2 * probe_count
    vmem = pl.BlockSpec(memory_space=pltpu.VMEM)
    rim = jax.ShapeDtypeStruct((probe_count, HALO), jnp.float32)
    return pl.pallas_call(
        element_kernel,
        out_shape=(jax.ShapeDtypeStruct(probes.shape, jnp.float32), rim, rim),
        in_specs=[vmem] * 7,
        out_specs=(vmem, vmem, vmem),
        scratch_shapes=[pltpu.VMEM((rows, WIDE), jnp.float32)],
        name="element_images",
    )(low, probes, high, connectivity, sensitivity, obs_weight, prior_weight.reshape(1, -1))


def rim_kernel(images_ref, lower_ref, upper_ref, sum_ref):
    node_count = images_ref.shape[1]
    sum_ref[...] = images_ref[...]
    sum_ref[:, :HALO] = images_ref[:, :HALO] + upper_ref[...]
    sum_ref[:, node_count - HALO :] = images_ref[:, node_count - HALO :] + lower_ref[...]


SUBLANES = 8
GROUP = 8
STAGES = 8
SLICE = 2.0**-8
PROBE_SLICES = 4
GRAM_SLICES = 5
INVERSE_SLICES = 4
FIRST_SLICES = 5


def power_of_two(value):
    return jnp.exp(value * math.log(2.0)).astype(jnp.bfloat16).astype(jnp.float32)


def bound_of(magnitude):
    return power_of_two(jnp.floor(jnp.log(magnitude) * (1.0 / math.log(2.0))) + 1.0)


def sliced(value, bound, count, late=None, late_at=0):
    sigma = bound * (1.5 * 2.0**16)
    slices = []
    for k in range(count):
        if late is not None and k == late_at:
            value = value + late
        piece = (value + sigma) - sigma
        slices.append(piece)
        value = value - piece
        sigma = sigma * SLICE
    return slices


def two_sum(a, b):
    total = a + b
    part = total - a
    return total, (a - (total - part)) + (b - part)


def added(left, right):
    total, error = two_sum(left[0], right[0])
    error = error + (left[1] + right[1])
    high = total + error
    return high, error - (high - total)


def add_levels(blocks, rows, columns, levels):
    high = low = None
    for level in range(levels):
        part = None
        for a in range(rows):
            b = level - a
            if 0 <= b < columns:
                part = blocks(a, b) if part is None else part + blocks(a, b)
        if high is None:
            high, low = part, jnp.zeros_like(part)
        else:
            high, error = two_sum(high, part)
            low = low + error
    total = high + low
    return total, low - (total - high)


def block_reader(products, size):
    return lambda a, b: products[a * size : (a + 1) * size, b * size : (b + 1) * size]


def gram_kernel(rows_ref, pair_ref):
    rows = rows_ref[...]
    size = rows.shape[0]
    bound = bound_of(jnp.max(jnp.abs(rows), axis=1, keepdims=True))
    stacked = jnp.concatenate(sliced(rows, bound, PROBE_SLICES), axis=0).astype(jnp.bfloat16)
    products = lax.dot_general(
        stacked, stacked, (((1,), (1,)), ((), ())), preferred_element_type=jnp.float32
    )
    high, low = add_levels(block_reader(products, size), PROBE_SLICES, PROBE_SLICES, 5)
    parts, double, _ = pair_ref.shape
    count = double // 2
    for part in range(parts):
        pair_ref[part, :count, :] = high[part * count : (part + 1) * count, :]
        pair_ref[part, count:, :] = low[part * count : (part + 1) * count, :]


def pairs_added(pairs):
    while len(pairs) > 1:
        joined = [added(a, b) for a, b in zip(pairs[::2], pairs[1::2])]
        pairs = joined + pairs[len(pairs) // 2 * 2 :]
    return pairs[0]


def halves(block):
    count = block.shape[0] // 2
    return block[:count, :], block[count:, :]


def sum_kernel(parts_ref, total_ref):
    high, low = pairs_added([halves(parts_ref[k]) for k in range(parts_ref.shape[0])])
    total_ref[...] = jnp.concatenate([high, low], axis=0)


def spread_kernel(own_ref, other_ref, copies_ref):
    high, low = added(halves(own_ref[...]), halves(other_ref[...]))
    total = jnp.concatenate([high, low], axis=0)
    for k in range(copies_ref.shape[0]):
        copies_ref[k] = total


def sum_spread_kernel(parts_ref, copies_ref):
    high, low = pairs_added([halves(parts_ref[k]) for k in range(parts_ref.shape[0])])
    total = jnp.concatenate([high, low], axis=0)
    for k in range(copies_ref.shape[0]):
        copies_ref[k] = total


def eliminate_group(tiles, pivots, at):
    shape = tiles[0].shape
    lane = lax.broadcasted_iota(jnp.int32, shape, 1)
    sub = lax.broadcasted_iota(jnp.int32, shape, 0)
    chosen = range(GROUP)
    columns = [[jnp.broadcast_to(tile[:, at + r : at + r + 1], shape) for r in chosen] for tile in tiles]
    entry = [
        [jnp.broadcast_to(columns[0][c][at + r : at + r + 1, :], shape) for c in chosen] for r in chosen
    ]
    rows = [jnp.broadcast_to(tiles[0][at + r : at + r + 1, :], shape) for r in chosen]
    factor = [[None] * GROUP for _ in chosen]
    scaled = []
    for s in chosen:
        over = 1.0 / entry[s][s]
        here = lane == at + s
        with_one = jnp.where(here, 1.0, rows[s])
        for r in range(s + 1, GROUP):
            factor[s][r] = entry[s][r] * over
            for c in range(r, GROUP):
                entry[r][c] = entry[r][c] - factor[s][r] * entry[s][c]
            rows[r] = jnp.where(here, 0.0, rows[r]) - factor[s][r] * with_one
        later = (lane > at + s) & (lane < at + GROUP)
        scaled.append(jnp.where(later, 0.0, with_one) * over)
    inside = (lane >= at) & (lane < at + GROUP)
    done = []
    for k, tile in enumerate(tiles):
        clear = inside
        if k == 0:
            below = sub >= at + GROUP
            clear = inside & below
        new = jnp.where(clear, 0.0, tile)
        own = list(columns[k])
        for s in chosen:
            for r in range(s + 1, GROUP):
                own[r] = own[r] - own[s] * factor[s][r]
        for s in chosen:
            value = jnp.where(below, own[s], 0.0) if k == 0 else own[s]
            new = new - value * scaled[s]
        if k == 0:
            for s in chosen:
                new = jnp.where(sub == at + s, rows[s], new)
                pivots = jnp.where(sub == at + s, entry[s][s], pivots)
        done.append(new)
    return done, pivots


def triangles(gram, tile_ref, pivot_ref):
    size = gram.shape[0]
    count = size // SUBLANES
    tiles = [gram[k * SUBLANES : (k + 1) * SUBLANES, :] for k in range(count)]

    def block(step, tiles):
        tiles = list(tiles)
        pivots = jnp.ones((SUBLANES, size), jnp.float32)
        for at in range(0, SUBLANES, GROUP):
            tiles, pivots = eliminate_group(tiles, pivots, at)
        place = pl.ds(pl.multiple_of(step * SUBLANES, SUBLANES), SUBLANES)
        tile_ref[place, :] = pltpu.roll(tiles[0], step * SUBLANES, 1)
        pivot_ref[place, :] = pivots
        tiles = [pltpu.roll(tile, size - SUBLANES, 1) for tile in tiles]
        return tuple(tiles[1:] + tiles[:1])

    each = count // STAGES
    for stage in range(STAGES):
        tiles = lax.fori_loop(stage * each, (stage + 1) * each, block, tuple(tiles))
        tiles = tiles[: len(tiles) - each]
    tile, pivot = tile_ref[...], pivot_ref[...]
    lane = lax.broadcasted_iota(jnp.int32, tile.shape, 1)
    row = lax.broadcasted_iota(jnp.int32, tile.shape, 0)
    root = lax.rsqrt(pivot)
    root = root * (1.5 - 0.5 * pivot * root * root)
    scaled = tile * root
    upper = jnp.where(lane > row, scaled, jnp.where(lane == row, pivot * root, 0.0))
    inverse = jnp.where(lane < row, scaled, jnp.where(lane == row, root, 0.0))
    return upper, inverse


def exact(a, b):
    return jnp.dot(a, b, precision=highest, preferred_element_type=jnp.float32)


def basis_kernel(scale, pair_ref, rows_ref, basis_ref, factor_ref, tile_ref, pivot_ref):
    parts, double, size = pair_ref.shape
    count = double // 2
    high = jnp.concatenate([pair_ref[k, :count, :] for k in range(parts)], axis=0)
    low = jnp.concatenate([pair_ref[k, count:, :] for k in range(parts)], axis=0)
    lane = lax.broadcasted_iota(jnp.int32, (size, size), 1)
    sub = lax.broadcasted_iota(jnp.int32, (size, size), 0)
    diagonal = jnp.where(lane == sub, high, 0.0)
    down = jnp.floor(jnp.log(jnp.max(diagonal, axis=1, keepdims=True)) * (0.5 / math.log(2.0)))
    across = jnp.floor(jnp.log(jnp.max(diagonal, axis=0, keepdims=True)) * (0.5 / math.log(2.0)))
    shrink = power_of_two(-down)
    shrink_across = power_of_two(-across)
    four = jnp.where(shrink > 0.0, 4.0, 8.0)
    high = high * shrink * shrink_across
    low = low * shrink * shrink_across

    upper_first, inverse_first = triangles(high, tile_ref, pivot_ref)

    gram_slices = sliced(high, four, GRAM_SLICES, late=low, late_at=3)
    bound = bound_of(jnp.max(jnp.abs(inverse_first), axis=1, keepdims=True))
    inverse_slices = sliced(inverse_first, bound, INVERSE_SLICES)
    gram_stack = jnp.concatenate(gram_slices, axis=0).astype(jnp.bfloat16)
    inverse_stack = jnp.concatenate(inverse_slices, axis=0).astype(jnp.bfloat16)
    products = lax.dot_general(
        gram_stack, inverse_stack, (((1,), (1,)), ((), ())), preferred_element_type=jnp.float32
    )
    lower_high, lower_low = add_levels(
        block_reader(products, size), GRAM_SLICES, INVERSE_SLICES, 6
    )
    lower_slices = sliced(lower_high, four, FIRST_SLICES, late=lower_low, late_at=3)
    lower_stack = jnp.concatenate(lower_slices, axis=1).astype(jnp.bfloat16)
    products = jnp.dot(inverse_stack, lower_stack, preferred_element_type=jnp.float32)
    gram_second, rest = add_levels(
        block_reader(products, size), INVERSE_SLICES, FIRST_SLICES, 5
    )
    gram_second = gram_second + rest

    upper_second, inverse_second = triangles(gram_second, tile_ref, pivot_ref)
    basis_first = exact(inverse_first, rows_ref[...] * shrink)
    basis = exact(inverse_second, basis_first)
    basis_ref[...] = basis * scale
    factor = exact(upper_second, upper_first)
    factor_ref[...] = factor * (power_of_two(across) * (1.0 / scale))


def in_vmem(kernel, name, out_shape, *operands, scratch=()):
    vmem = pl.BlockSpec(memory_space=pltpu.VMEM)
    single = not isinstance(out_shape, tuple)
    return pl.pallas_call(
        kernel,
        out_shape=out_shape,
        in_specs=[vmem] * len(operands),
        out_specs=vmem if single else tuple(vmem for _ in out_shape),
        scratch_shapes=scratch,
        name=name,
    )(*operands)


def orthonormal(rows, scale):
    size = rows.shape[0]
    parts = lax.axis_size("probe")
    count = 2 * size // parts
    places = lax.axis_size("space")
    pair = jax.ShapeDtypeStruct((parts, count, size), jnp.float32)
    one = jax.ShapeDtypeStruct((count, size), jnp.float32)
    levels = places // CORES
    copies = jax.ShapeDtypeStruct((levels, count, size), jnp.float32)
    gram = in_vmem(gram_kernel, "gram", pair, rows)
    gram = lax.all_to_all(gram, "probe", 0, 0, tiled=True)
    own = in_vmem(sum_kernel, "probe_sum", one, gram)
    other = lax.ppermute(own, "space", [(k, k ^ 1) for k in range(places)])
    spread = in_vmem(spread_kernel, "core_sum", copies, own, other)
    groups = [[core + CORES * k for k in range(levels)] for core in range(CORES)]
    spread = lax.all_to_all(spread, "space", 0, 0, tiled=True, axis_index_groups=groups)
    whole = in_vmem(sum_spread_kernel, "space_sum", pair, spread)
    whole = lax.all_to_all(whole, "probe", 0, 0, tiled=True)
    return in_vmem(
        functools.partial(basis_kernel, scale), "basis",
        (
            jax.ShapeDtypeStruct(rows.shape, jnp.float32),
            jax.ShapeDtypeStruct((size, size), jnp.float32),
        ),
        whole, rows,
        scratch=(pltpu.VMEM((size, size), jnp.float32),) * 2,
    )


def on_device(probes, sensitivity, obs_weight, prior_weight, connectivity):
    node_count = probes.shape[1]
    low = shifted(probes[:, node_count - HALO :], "space", 1)
    high = shifted(probes[:, :HALO], "space", -1)
    images, lower, upper = element_images(
        low, probes, high, connectivity, sensitivity, obs_weight, prior_weight
    )
    lower_rim = shifted(lower, "space", -1)
    upper_rim = shifted(upper, "space", 1)
    images = in_vmem(
        rim_kernel, "rims", jax.ShapeDtypeStruct(images.shape, jnp.float32),
        images, lower_rim, upper_rim,
    )
    scale = math.sqrt(float(node_count * lax.axis_size("space")))
    rows = lax.all_to_all(images, "probe", 1, 0, tiled=True)
    basis, factor = orthonormal(rows, scale)
    return lax.all_to_all(basis, "probe", 0, 1, tiled=True), factor


def solution(mesh):
    return jax.shard_map(
        on_device,
        mesh=mesh,
        in_specs=(
            P("probe", "space"),
            P(None, None, "space"),
            P(None, "space"),
            P("space"),
            P(None, "space"),
        ),
        out_specs=(P("probe", "space"), P()),
        check_vma=False,
    )
```

```python
import functools
import math

import jax
import jax.numpy as jnp
from jax import lax
from jax.experimental import pallas as pl
from jax.experimental.pallas import tpu as pltpu
from jax.sharding import PartitionSpec as P

HALO = 128
LANES = 128
WIDE = 256
CORES = 2
GRANT = 16 * 2**20
TOGETHER = 8

highest = lax.Precision.HIGHEST


def shifted(block, axis, distance):
    devices = range(lax.axis_size(axis))
    route = [(i - distance, i) for i in devices if i - distance in devices]
    return lax.ppermute(block, axis, route)


def selected(candidates, place, bit):
    if len(candidates) == 1:
        return candidates[0]()
    span = 1 << bit
    if len(candidates) <= span:
        return selected(candidates, place, bit - 1)
    low = selected(candidates[:span], place, bit - 1)
    high = selected(candidates[span:], place, bit - 1)
    return jnp.where((place & span) != 0, high, low)


def element_kernel(
    below_ref, probes_ref, above_ref, connectivity_ref, sensitivity_ref, weight_ref, prior_ref,
    images_ref, lower_ref, upper_ref, total_ref, low_ref, high_ref, low_done, high_done,
):
    low = pltpu.make_async_copy(below_ref, low_ref, low_done)
    high = pltpu.make_async_copy(above_ref, high_ref, high_done)
    low.start()
    high.start()
    low.wait()
    high.wait()
    probe_count, node_count = probes_ref.shape
    corner_count, element_count = connectivity_ref.shape
    gauss_count = sensitivity_ref.shape[0]
    tiles = node_count // LANES + 2
    blocks = tiles * LANES // WIDE
    packed = 2 * probe_count
    thirds = -(-blocks // 2)

    def tile(k):
        if k == 0:
            return low_ref[...]
        if k == tiles - 1:
            return high_ref[...]
        return probes_ref[:, (k - 1) * LANES : k * LANES]

    total_ref[...] = jnp.zeros_like(total_ref)
    row = lax.broadcasted_iota(jnp.int32, (WIDE, LANES), 0).astype(jnp.float32).astype(jnp.bfloat16)
    lower_half = lax.broadcasted_iota(jnp.int32, (packed, LANES), 0) >= probe_count
    lower_half = jnp.where(lower_half, 1.0, 0.0)
    one = jnp.ones((WIDE, LANES), jnp.bfloat16)
    none = jnp.zeros((WIDE, LANES), jnp.bfloat16)
    zero = jnp.zeros((packed, LANES), jnp.bfloat16)
    top_bit = (tiles - 1).bit_length() - 1

    def columns_of(step):
        return pl.ds(pl.multiple_of(step * LANES, LANES), LANES)

    def node_of(corner, step):
        return jnp.broadcast_to(
            connectivity_ref[corner : corner + 1, columns_of(step)], (probe_count, LANES)
        )

    def gather(corner, step):
        node = node_of(corner, step)
        lane = node & (LANES - 1)
        picks = [
            functools.partial(
                lambda k, at: jnp.take_along_axis(tile(k), at, axis=1, mode="promise_in_bounds"),
                k, lane,
            )
            for k in range(tiles)
        ]
        return selected(picks, lax.shift_right_logical(node, 7), top_bit)

    def pull(gathered, step):
        columns = columns_of(step)
        observed = []
        for gauss in range(gauss_count):
            value = gathered[0] * sensitivity_ref[gauss, 0:1, columns]
            for corner in range(1, corner_count):
                value = value + gathered[corner] * sensitivity_ref[gauss, corner : corner + 1, columns]
            observed.append(value * weight_ref[gauss : gauss + 1, columns])
        pulled = []
        for corner in range(corner_count):
            value = observed[0] * sensitivity_ref[0, corner : corner + 1, columns]
            for gauss in range(1, gauss_count):
                value = value + observed[gauss] * sensitivity_ref[gauss, corner : corner + 1, columns]
            pulled.append(value)
        return tuple(pulled)

    def operands(value, corner, step):
        first = value.astype(jnp.bfloat16).astype(jnp.float32)
        rest = value - first
        second = rest.astype(jnp.bfloat16).astype(jnp.float32)
        third = rest - second
        heads = jnp.concatenate([first, second], axis=0).astype(jnp.bfloat16)
        tails = jnp.concatenate([third, third], axis=0).astype(jnp.bfloat16)
        node = node_of(corner, step)
        place = lax.shift_right_logical(node, 8).astype(jnp.float32)
        place = jnp.concatenate([place, place], axis=0)
        offset = (place - lower_half).astype(jnp.bfloat16)
        place = place.astype(jnp.bfloat16)
        parts = []
        for k in range(blocks):
            here = place == jnp.full((packed, LANES), k, jnp.bfloat16)
            parts.append(jnp.where(here, heads, zero))
        for k in range(thirds):
            here = offset == jnp.full((packed, LANES), 2 * k, jnp.bfloat16)
            parts.append(jnp.where(here, tails, zero))
        lane = (node & (WIDE - 1)).astype(jnp.float32)
        lane = jnp.concatenate([lane, lane], axis=0).astype(jnp.bfloat16)
        lane = jnp.concatenate([lane] * (WIDE // packed), axis=0)
        return jnp.concatenate(parts, axis=0), jnp.where(row == lane, one, none)

    last = element_count // LANES - 1

    def trip(step, pulled):
        ahead = jnp.minimum(step + 1, last)
        gathered = []
        for group in range(0, corner_count, TOGETHER):
            left, right = [], []
            for corner in range(group, group + TOGETHER):
                gathered.append(gather(corner, ahead))
                a, b = operands(pulled[corner], corner, step)
                left.append(a)
                right.append(b)
            total_ref[...] += lax.dot_general(
                jnp.concatenate(left, axis=1), jnp.concatenate(right, axis=1),
                (((1,), (1,)), ((), ())), preferred_element_type=jnp.float32,
            )
        return pull(gathered, ahead)

    pulled = pull([gather(corner, 0) for corner in range(corner_count)], 0)
    lax.fori_loop(0, last + 1, trip, pulled)

    for block in range(blocks):
        at = block * packed
        tail = blocks * packed + block * probe_count
        value = total_ref[tail : tail + probe_count, :]
        value = value + total_ref[at + probe_count : at + packed, :]
        value = value + total_ref[at : at + probe_count, :]
        for half in range(WIDE // LANES):
            k = block * (WIDE // LANES) + half
            part = value[:, half * LANES : (half + 1) * LANES]
            if k == 0:
                lower_ref[...] = part
            elif k == tiles - 1:
                upper_ref[...] = part
            else:
                span = slice((k - 1) * LANES, k * LANES)
                images_ref[:, span] = part + prior_ref[:, span] * probes_ref[:, span]


def element_images(low, probes, high, connectivity, sensitivity, obs_weight, prior_weight):
    probe_count, node_count = probes.shape
    corner_count = connectivity.shape[0]
    blocks = (node_count + 2 * HALO) // WIDE
    rows = (blocks + -(-blocks // 2)) * 2 * probe_count
    vmem = pl.BlockSpec(memory_space=pltpu.VMEM)
    away = pl.BlockSpec(memory_space=pl.ANY)
    rim = jax.ShapeDtypeStruct((probe_count, HALO), jnp.float32)
    return pl.pallas_call(
        element_kernel,
        out_shape=(jax.ShapeDtypeStruct(probes.shape, jnp.float32), rim, rim),
        in_specs=[away, vmem, away, vmem, vmem, vmem, vmem],
        out_specs=(vmem, vmem, vmem),
        scratch_shapes=[
            pltpu.VMEM((rows, WIDE), jnp.float32),
            pltpu.VMEM((probe_count, HALO), jnp.float32),
            pltpu.VMEM((probe_count, HALO), jnp.float32),
            pltpu.SemaphoreType.DMA,
            pltpu.SemaphoreType.DMA,
        ],
        compiler_params=pltpu.CompilerParams(vmem_limit_bytes=GRANT),
        name="element_images",
    )(low, probes, high, connectivity, sensitivity, obs_weight, prior_weight.reshape(1, -1))


def rim_kernel(images_ref, low_ref, up_ref, sum_ref, lower_ref, upper_ref, low_done, up_done):
    low = pltpu.make_async_copy(low_ref, lower_ref, low_done)
    up = pltpu.make_async_copy(up_ref, upper_ref, up_done)
    low.start()
    up.start()
    low.wait()
    up.wait()
    node_count = images_ref.shape[1]
    sum_ref[...] = images_ref[...]
    sum_ref[:, :HALO] = images_ref[:, :HALO] + upper_ref[...]
    sum_ref[:, node_count - HALO :] = images_ref[:, node_count - HALO :] + lower_ref[...]


SUBLANES = 8
GROUP = 8
STAGES = 8
SLICE = 2.0**-8
PROBE_SLICES = 4
GRAM_SLICES = 5
INVERSE_SLICES = 4
FIRST_SLICES = 5


def power_of_two(value):
    return jnp.exp(value * math.log(2.0)).astype(jnp.bfloat16).astype(jnp.float32)


def bound_of(magnitude):
    return power_of_two(jnp.floor(jnp.log(magnitude) * (1.0 / math.log(2.0))) + 1.0)


def sliced(value, bound, count, late=None, late_at=0):
    sigma = bound * (1.5 * 2.0**16)
    slices = []
    for k in range(count):
        if late is not None and k == late_at:
            value = value + late
        piece = (value + sigma) - sigma
        slices.append(piece)
        value = value - piece
        sigma = sigma * SLICE
    return slices


def two_sum(a, b):
    total = a + b
    part = total - a
    return total, (a - (total - part)) + (b - part)


def added(left, right):
    total, error = two_sum(left[0], right[0])
    error = error + (left[1] + right[1])
    high = total + error
    return high, error - (high - total)


def add_levels(blocks, rows, columns, levels):
    high = low = None
    for level in range(levels):
        part = None
        for a in range(rows):
            b = level - a
            if 0 <= b < columns:
                part = blocks(a, b) if part is None else part + blocks(a, b)
        if high is None:
            high, low = part, jnp.zeros_like(part)
        else:
            high, error = two_sum(high, part)
            low = low + error
    total = high + low
    return total, low - (total - high)


def block_reader(products, size):
    return lambda a, b: products[a * size : (a + 1) * size, b * size : (b + 1) * size]


def gram_kernel(rows_ref, pair_ref):
    rows = rows_ref[...]
    size = rows.shape[0]
    bound = bound_of(jnp.max(jnp.abs(rows), axis=1, keepdims=True))
    stacked = jnp.concatenate(sliced(rows, bound, PROBE_SLICES), axis=0).astype(jnp.bfloat16)
    products = lax.dot_general(
        stacked, stacked, (((1,), (1,)), ((), ())), preferred_element_type=jnp.float32
    )
    high, low = add_levels(block_reader(products, size), PROBE_SLICES, PROBE_SLICES, 5)
    parts, double, _ = pair_ref.shape
    count = double // 2
    for part in range(parts):
        pair_ref[part, :count, :] = high[part * count : (part + 1) * count, :]
        pair_ref[part, count:, :] = low[part * count : (part + 1) * count, :]


def pairs_added(pairs):
    while len(pairs) > 1:
        joined = [added(a, b) for a, b in zip(pairs[::2], pairs[1::2])]
        pairs = joined + pairs[len(pairs) // 2 * 2 :]
    return pairs[0]


def halves(block):
    count = block.shape[0] // 2
    return block[:count, :], block[count:, :]


def sum_kernel(parts_ref, total_ref):
    high, low = pairs_added([halves(parts_ref[k]) for k in range(parts_ref.shape[0])])
    total_ref[...] = jnp.concatenate([high, low], axis=0)


def fetched(source_ref, target_ref, semaphore):
    copy = pltpu.make_async_copy(source_ref, target_ref, semaphore)
    copy.start()
    copy.wait()


def spread_kernel(own_ref, away_ref, copies_ref, other_ref, semaphore):
    fetched(away_ref, other_ref, semaphore)
    high, low = added(halves(own_ref[...]), halves(other_ref[...]))
    total = jnp.concatenate([high, low], axis=0)
    for k in range(copies_ref.shape[0]):
        copies_ref[k] = total


def sum_spread_kernel(parts_ref, copies_ref):
    high, low = pairs_added([halves(parts_ref[k]) for k in range(parts_ref.shape[0])])
    total = jnp.concatenate([high, low], axis=0)
    for k in range(copies_ref.shape[0]):
        copies_ref[k] = total


def eliminate_group(tiles, pivots, at):
    shape = tiles[0].shape
    lane = lax.broadcasted_iota(jnp.int32, shape, 1)
    sub = lax.broadcasted_iota(jnp.int32, shape, 0)
    chosen = range(GROUP)
    columns = [[jnp.broadcast_to(tile[:, at + r : at + r + 1], shape) for r in chosen] for tile in tiles]
    entry = [
        [jnp.broadcast_to(columns[0][c][at + r : at + r + 1, :], shape) for c in chosen] for r in chosen
    ]
    rows = [jnp.broadcast_to(tiles[0][at + r : at + r + 1, :], shape) for r in chosen]
    factor = [[None] * GROUP for _ in chosen]
    scaled = []
    for s in chosen:
        over = 1.0 / entry[s][s]
        here = lane == at + s
        with_one = jnp.where(here, 1.0, rows[s])
        for r in range(s + 1, GROUP):
            factor[s][r] = entry[s][r] * over
            for c in range(r, GROUP):
                entry[r][c] = entry[r][c] - factor[s][r] * entry[s][c]
            rows[r] = jnp.where(here, 0.0, rows[r]) - factor[s][r] * with_one
        later = (lane > at + s) & (lane < at + GROUP)
        scaled.append(jnp.where(later, 0.0, with_one) * over)
    inside = (lane >= at) & (lane < at + GROUP)
    done = []
    for k, tile in enumerate(tiles):
        clear = inside
        if k == 0:
            below = sub >= at + GROUP
            clear = inside & below
        new = jnp.where(clear, 0.0, tile)
        own = list(columns[k])
        for s in chosen:
            for r in range(s + 1, GROUP):
                own[r] = own[r] - own[s] * factor[s][r]
        for s in chosen:
            value = jnp.where(below, own[s], 0.0) if k == 0 else own[s]
            new = new - value * scaled[s]
        if k == 0:
            for s in chosen:
                new = jnp.where(sub == at + s, rows[s], new)
                pivots = jnp.where(sub == at + s, entry[s][s], pivots)
        done.append(new)
    return done, pivots


def triangles(gram, tile_ref, pivot_ref):
    size = gram.shape[0]
    count = size // SUBLANES
    tiles = [gram[k * SUBLANES : (k + 1) * SUBLANES, :] for k in range(count)]

    def block(step, tiles):
        tiles = list(tiles)
        pivots = jnp.ones((SUBLANES, size), jnp.float32)
        for at in range(0, SUBLANES, GROUP):
            tiles, pivots = eliminate_group(tiles, pivots, at)
        place = pl.ds(pl.multiple_of(step * SUBLANES, SUBLANES), SUBLANES)
        tile_ref[place, :] = pltpu.roll(tiles[0], step * SUBLANES, 1)
        pivot_ref[place, :] = pivots
        tiles = [pltpu.roll(tile, size - SUBLANES, 1) for tile in tiles]
        return tuple(tiles[1:] + tiles[:1])

    each = count // STAGES
    for stage in range(STAGES):
        tiles = lax.fori_loop(stage * each, (stage + 1) * each, block, tuple(tiles))
        tiles = tiles[: len(tiles) - each]
    tile, pivot = tile_ref[...], pivot_ref[...]
    lane = lax.broadcasted_iota(jnp.int32, tile.shape, 1)
    row = lax.broadcasted_iota(jnp.int32, tile.shape, 0)
    root = lax.rsqrt(pivot)
    root = root * (1.5 - 0.5 * pivot * root * root)
    scaled = tile * root
    upper = jnp.where(lane > row, scaled, jnp.where(lane == row, pivot * root, 0.0))
    inverse = jnp.where(lane < row, scaled, jnp.where(lane == row, root, 0.0))
    return upper, inverse


def exact(a, b):
    return jnp.dot(a, b, precision=highest, preferred_element_type=jnp.float32)


def basis_kernel(scale, pair_ref, rows_ref, basis_ref, factor_ref, tile_ref, pivot_ref):
    parts, double, size = pair_ref.shape
    count = double // 2
    high = jnp.concatenate([pair_ref[k, :count, :] for k in range(parts)], axis=0)
    low = jnp.concatenate([pair_ref[k, count:, :] for k in range(parts)], axis=0)
    lane = lax.broadcasted_iota(jnp.int32, (size, size), 1)
    sub = lax.broadcasted_iota(jnp.int32, (size, size), 0)
    diagonal = jnp.where(lane == sub, high, 0.0)
    down = jnp.floor(jnp.log(jnp.max(diagonal, axis=1, keepdims=True)) * (0.5 / math.log(2.0)))
    across = jnp.floor(jnp.log(jnp.max(diagonal, axis=0, keepdims=True)) * (0.5 / math.log(2.0)))
    shrink = power_of_two(-down)
    shrink_across = power_of_two(-across)
    four = jnp.where(shrink > 0.0, 4.0, 8.0)
    high = high * shrink * shrink_across
    low = low * shrink * shrink_across

    upper_first, inverse_first = triangles(high, tile_ref, pivot_ref)

    gram_slices = sliced(high, four, GRAM_SLICES, late=low, late_at=3)
    bound = bound_of(jnp.max(jnp.abs(inverse_first), axis=1, keepdims=True))
    inverse_slices = sliced(inverse_first, bound, INVERSE_SLICES)
    gram_stack = jnp.concatenate(gram_slices, axis=0).astype(jnp.bfloat16)
    inverse_stack = jnp.concatenate(inverse_slices, axis=0).astype(jnp.bfloat16)
    products = lax.dot_general(
        gram_stack, inverse_stack, (((1,), (1,)), ((), ())), preferred_element_type=jnp.float32
    )
    lower_high, lower_low = add_levels(
        block_reader(products, size), GRAM_SLICES, INVERSE_SLICES, 6
    )
    lower_slices = sliced(lower_high, four, FIRST_SLICES, late=lower_low, late_at=3)
    lower_stack = jnp.concatenate(lower_slices, axis=1).astype(jnp.bfloat16)
    products = jnp.dot(inverse_stack, lower_stack, preferred_element_type=jnp.float32)
    gram_second, rest = add_levels(
        block_reader(products, size), INVERSE_SLICES, FIRST_SLICES, 5
    )
    gram_second = gram_second + rest

    upper_second, inverse_second = triangles(gram_second, tile_ref, pivot_ref)
    basis_first = exact(inverse_first, rows_ref[...] * shrink)
    basis = exact(inverse_second, basis_first)
    basis_ref[...] = basis * scale
    factor = exact(upper_second, upper_first)
    factor_ref[...] = factor * (power_of_two(across) * (1.0 / scale))


def in_vmem(kernel, name, out_shape, *operands, scratch=(), away=()):
    vmem = pl.BlockSpec(memory_space=pltpu.VMEM)
    single = not isinstance(out_shape, tuple)
    return pl.pallas_call(
        kernel,
        out_shape=out_shape,
        in_specs=[
            pl.BlockSpec(memory_space=pl.ANY) if k in away else vmem for k in range(len(operands))
        ],
        out_specs=vmem if single else tuple(vmem for _ in out_shape),
        scratch_shapes=scratch,
        compiler_params=pltpu.CompilerParams(vmem_limit_bytes=GRANT),
        name=name,
    )(*operands)


def orthonormal(rows, scale):
    size = rows.shape[0]
    parts = lax.axis_size("probe")
    count = 2 * size // parts
    places = lax.axis_size("space")
    pair = jax.ShapeDtypeStruct((parts, count, size), jnp.float32)
    one = jax.ShapeDtypeStruct((count, size), jnp.float32)
    levels = places // CORES
    copies = jax.ShapeDtypeStruct((levels, count, size), jnp.float32)
    gram = in_vmem(gram_kernel, "gram", pair, rows)
    gram = lax.all_to_all(gram, "probe", 0, 0, tiled=True)
    own = in_vmem(sum_kernel, "probe_sum", one, gram)
    other = lax.ppermute(own, "space", [(k, k ^ 1) for k in range(places)])
    spread = in_vmem(spread_kernel, "core_sum", copies, own, other, away=(1,),
        scratch=(pltpu.VMEM((count, size), jnp.float32), pltpu.SemaphoreType.DMA))
    groups = [[core + CORES * k for k in range(levels)] for core in range(CORES)]
    spread = lax.all_to_all(spread, "space", 0, 0, tiled=True, axis_index_groups=groups)
    whole = in_vmem(sum_spread_kernel, "space_sum", pair, spread)
    whole = lax.all_to_all(whole, "probe", 0, 0, tiled=True)
    return in_vmem(
        functools.partial(basis_kernel, scale), "basis",
        (
            jax.ShapeDtypeStruct(rows.shape, jnp.float32),
            jax.ShapeDtypeStruct((size, size), jnp.float32),
        ),
        whole, rows,
        scratch=(pltpu.VMEM((size, size), jnp.float32),) * 2,
    )


def on_device(probes, sensitivity, obs_weight, prior_weight, connectivity):
    node_count = probes.shape[1]
    low = shifted(probes[:, node_count - HALO :], "space", 1)
    high = shifted(probes[:, :HALO], "space", -1)
    images, lower, upper = element_images(
        low, probes, high, connectivity, sensitivity, obs_weight, prior_weight
    )
    lower_rim = shifted(lower, "space", -1)
    upper_rim = shifted(upper, "space", 1)
    images = in_vmem(
        rim_kernel, "rims", jax.ShapeDtypeStruct(images.shape, jnp.float32),
        images, lower_rim, upper_rim, away=(1, 2),
        scratch=(pltpu.VMEM(lower_rim.shape, jnp.float32),) * 2 + (pltpu.SemaphoreType.DMA,) * 2,
    )
    scale = math.sqrt(float(node_count * lax.axis_size("space")))
    rows = lax.all_to_all(images, "probe", 1, 0, tiled=True)
    basis, factor = orthonormal(rows, scale)
    return lax.all_to_all(basis, "probe", 0, 1, tiled=True), factor


def solution(mesh):
    return jax.shard_map(
        on_device,
        mesh=mesh,
        in_specs=(
            P("probe", "space"),
            P(None, None, "space"),
            P(None, "space"),
            P("space"),
            P(None, "space"),
        ),
        out_specs=(P("probe", "space"), P()),
        check_vma=False,
    )
```
